32 devices in a mesh: tile: 4 (over y, core), dp: 8 (over z, x).
Axes of the slice: x: 2, y: 2, z: 4, core: 2. Of those that a mesh axis runs over, the one named last changes fastest.
Arguments:
- observed: float32 [8, 2, 8, 32], P('dp', None, 'tile'), may hold values from -6 to 6
- targets: float32 [8, 2, 8, 32], P('dp', None, 'tile'), may hold values from -6 to 6
- pixel_mask: int32 [8, 2, 8, 32], P('dp', None, 'tile'), may hold values 0 or 1
- lengths: int32 [8], P('dp'), may hold values from 1 to 2, as said below
- step_count: int32 [1], replicated, may hold values from 2 to 20
- kernels: float32 [1, 12800, 1024], P(None, 'dp'), may hold values from -0.0546875 to 0.0546875
- kernel_moment: float32 [1, 12800, 1024], P(None, 'dp'), may hold values from -7.6293945e-06 to 7.6293945e-06
- kernel_second: float32 [1, 12800, 1024], P(None, 'dp'), may hold values from 1.9073486e-12 to 7.6293945e-12
- norm_params: float32 [2, 1, 1024], replicated
- norm_moment: float32 [2, 1, 1024], replicated, may hold values from -1.5258789e-05 to 1.5258789e-05
- norm_second: float32 [2, 1, 1024], replicated, may hold values from 7.6293945e-12 to 3.0517578e-11
- end_params: float32 [3, 256], replicated
- end_moment: float32 [3, 256], replicated, may hold values from -7.6293945e-05 to 7.6293945e-05
- end_second: float32 [3, 256], replicated, may hold values from 1.9073486e-10 to 7.6293943e-10
- head_bias: float32 [1], replicated, may hold values from -3 to 3
- head_moment: float32 [1], replicated, may hold values from -0.0546875 to 0.0546875
- head_second: float32 [1], replicated, may hold values from 7.6293945e-05 to 0.00030517578
- hidden_init: float32 [1, 8, 8, 32, 256], P(None, 'dp', 'tile'), may hold values from -0.9 to 0.9
- cells_init: float32 [1, 8, 8, 32, 256], P(None, 'dp', 'tile'), may hold values from -5 to 5
Outputs:
- loss_value: float32 [], replicated
- grad_norm: float32 [], replicated
- kernels_new: float32 [1, 12800, 1024], P(None, 'dp')
- kernel_moment_new: float32 [1, 12800, 1024], P(None, 'dp')
- kernel_second_new: float32 [1, 12800, 1024], P(None, 'dp')
- norm_new: float32 [2, 1, 1024], replicated
- norm_moment_new: float32 [2, 1, 1024], replicated
- norm_second_new: float32 [2, 1, 1024], replicated
- end_new: float32 [3, 256], replicated
- end_moment_new: float32 [3, 256], replicated
- end_second_new: float32 [3, 256], replicated
- head_new: float32 [1], replicated
- head_moment_new: float32 [1], replicated
- head_second_new: float32 [1], replicated
- hidden_final: float32 [1, 8, 8, 32, 256], P(None, 'dp', 'tile')
- cells_final: float32 [1, 8, 8, 32, 256], P(None, 'dp', 'tile')
The draws below stay inside these ranges and needn't reach their ends.
Inputs may be any that keep to these rules, and one draw needn't show every extreme that they name: `lengths`: some stream has all 2 frames counting and some only one.
All inputs are finite; a program needn't handle non-finite values. No bound on the sum of `pixel_mask` on one device may be relied on, other than what follows from the above.
Results may differ from the reference program's by a relative error of at most 0.0003.
The reference program's roundings to bfloat16 on the way count: a program that leaves them out, or rounds other values in their place, can miss the bound.
Values may be sent and summed in bfloat16 or wider, within the bound.
No kernel may reach another device: no remote copies, remote signals or barrier semaphores. Data moves between devices by JAX's collectives and lax.ppermute only.
A program may use at most 192 MiB of HBM per device.

```python
import math
import jax
import jax.numpy as jnp
from jax import lax

HID_DIM = 256
GATE_DIM = 1024
IN_DIM = 512
KERNEL = 5
GROUP_SIZE = 64
LAYERS = 1
FRAMES = 2
COLUMNS = 32
STREAMS = 8
HEIGHT = 8


def draw_lengths(key, part):
    first, second = jax.random.split(key)
    counts = jax.random.randint(first, (STREAMS,), 1, FRAMES + 1)
    places = jax.random.permutation(second, STREAMS)
    counts = counts.at[places[0]].set(FRAMES)
    counts = counts.at[places[1]].set(1)
    return counts.astype(jnp.int32)


def draw_norm_params(key, part):
    first, second = jax.random.split(key)
    gains = jax.random.uniform(first, (1, LAYERS, GATE_DIM), jnp.float32, 0.6, 1.4)
    shifts = 0.4 * jax.random.normal(second, (1, LAYERS, GATE_DIM), jnp.float32)
    return jnp.concatenate([gains, shifts], axis=0)


def draw_end_params(key, part):
    values = jax.random.normal(key, (3, HID_DIM), jnp.float32)
    scales = jnp.array([1.0, 0.5, 2.0 * HID_DIM ** (-0.5)], jnp.float32)
    return values * scales[:, None]


def set_ends(drawn, stream_key, low, top_value):
    spot = [jax.random.randint(jax.random.fold_in(stream_key, axis), (), 0, length) for axis, length in enumerate(drawn.shape)]
    widest = drawn.shape.index(max(drawn.shape))
    next_to = spot[:widest] + [(spot[widest] + 1) % drawn.shape[widest]] + spot[widest + 1:]
    return drawn.at[tuple(spot)].set(low).at[tuple(next_to)].set(top_value)


def shard_levels(stream_key, shape, cuts, least, largest):
    loudness, own = 1.0, jax.random.fold_in(stream_key, 6)
    for position, blocks in cuts:
        heights = jnp.exp(jax.random.uniform(jax.random.fold_in(own, position), (blocks,), jnp.float32, least / len(cuts), largest / len(cuts)))
        loudness = loudness * jnp.repeat(heights, shape[position] // blocks).reshape([-1 if axis == position else 1 for axis in range(len(shape))])
    return loudness


def normal_values(rng, shape, scale, reach, cuts=(), kind=jnp.bfloat16):
    values = scale * jax.random.normal(rng, shape, jnp.float32)
    if cuts:
        values = values * shard_levels(rng, shape, cuts, -0.22, 0.18)
    return jnp.clip(values, -reach, reach).astype(kind)


def setup_inputs(seed: int = 0) -> dict:
    key_list = jax.random.split(jax.random.key(seed), 20)
    return {
        "observed": normal_values(key_list[0], (STREAMS, FRAMES, HEIGHT, COLUMNS), 1.0, 6.0, ((0, 8), (2, 4)), jnp.float32),
        "targets": normal_values(key_list[1], (STREAMS, FRAMES, HEIGHT, COLUMNS), 1.0, 6.0, ((0, 8), (2, 4)), jnp.float32),
        "pixel_mask": set_ends((jax.random.randint(key_list[2], (STREAMS, FRAMES, HEIGHT, COLUMNS), 0, 4) < 3).astype(jnp.int32), jax.random.fold_in(key_list[2], 1), 0, 1),
        "lengths": draw_lengths(jax.random.fold_in(key_list[19], 71), 0),
        "step_count": jax.random.randint(key_list[4], (1,), 2, 21).astype(jnp.int32),
        "kernels": normal_values(key_list[5], (LAYERS, KERNEL * KERNEL * IN_DIM, GATE_DIM), (KERNEL * KERNEL * IN_DIM) ** -0.5, 0.0546875, ((1, 8),), jnp.float32),
        "kernel_moment": normal_values(key_list[6], (LAYERS, KERNEL * KERNEL * IN_DIM, GATE_DIM), (40000 * LAYERS * KERNEL * KERNEL * IN_DIM * GATE_DIM) ** -0.5, 7.62939453125e-06, ((1, 8),), jnp.float32),
        "kernel_second": jnp.clip(jnp.exp(math.log(7.62939451198763e-12) - 1.3862944 * jax.random.uniform(key_list[7], (LAYERS, KERNEL * KERNEL * IN_DIM, GATE_DIM), jnp.float32) ** shard_levels(key_list[7], (LAYERS, KERNEL * KERNEL * IN_DIM, GATE_DIM), ((1, 8),), -0.2, 0.2)), 1.9073486279969076e-12, 7.62939451198763e-12),
        "norm_params": draw_norm_params(jax.random.fold_in(key_list[19], 71), 0),
        "norm_moment": normal_values(key_list[9], (2, LAYERS, GATE_DIM), (10000 * LAYERS * KERNEL * KERNEL * IN_DIM * GATE_DIM) ** -0.5, 1.52587890625e-05, (), jnp.float32),
        "norm_second": jnp.clip(jnp.exp(jax.random.uniform(key_list[10], (2, LAYERS, GATE_DIM), jnp.float32, math.log(7.62939451198763e-12), math.log(3.051757804795052e-11))), 7.62939451198763e-12, 3.051757804795052e-11),
        "end_params": draw_end_params(jax.random.fold_in(key_list[19], 71), 0),
        "end_moment": normal_values(key_list[12], (3, HID_DIM), (400 * LAYERS * KERNEL * KERNEL * IN_DIM * GATE_DIM) ** -0.5, 7.62939453125e-05, (), jnp.float32),
        "end_second": jnp.clip(jnp.exp(jax.random.uniform(key_list[13], (3, HID_DIM), jnp.float32, math.log(1.9073485846288207e-10), math.log(7.629394338515283e-10))), 1.9073485846288207e-10, 7.629394338515283e-10),
        "head_bias": normal_values(key_list[14], (1,), 0.5, 3.0, (), jnp.float32),
        "head_moment": normal_values(key_list[15], (1,), (LAYERS * KERNEL * KERNEL * IN_DIM * GATE_DIM // 1000) ** -0.5, 0.0546875, (), jnp.float32),
        "head_second": jnp.clip(jnp.exp(jax.random.uniform(key_list[16], (1,), jnp.float32, math.log(7.62939453125e-05), math.log(0.00030517578))), 7.62939453125e-05, 0.00030517578),
        "hidden_init": jnp.clip(jax.random.uniform(key_list[17], (LAYERS, STREAMS, HEIGHT, COLUMNS, HID_DIM), jnp.float32, -0.9, 0.9) * shard_levels(key_list[17], (LAYERS, STREAMS, HEIGHT, COLUMNS, HID_DIM), ((1, 8), (2, 4)), -0.4, 0.0), -0.9, 0.9),
        "cells_init": normal_values(key_list[18], (LAYERS, STREAMS, HEIGHT, COLUMNS, HID_DIM), 1.0, 5.0, ((1, 8), (2, 4)), jnp.float32),
    }


@jax.custom_vjp
def low(v):
    return lax.optimization_barrier(v.astype(jnp.bfloat16)).astype(jnp.float32)

@jax.custom_vjp
def low_back(v):
    return v

def low_keep(v):
    return (low(v), None)

def low_pass(kept, grad):
    return (grad,)

def back_keep(v):
    return (v, None)

def back_low(kept, grad):
    return (low(grad),)
low.defvjp(low_keep, low_pass)
low_back.defvjp(back_keep, back_low)
clip_limit = 0.005
small_rate = 0.1

def group_norm(gates, gain, shift):
    full_shape = gates.shape
    grouped = gates.reshape(full_shape[:-1] + (full_shape[-1] // GROUP_SIZE, GROUP_SIZE))
    centred = grouped - lax.optimization_barrier(jnp.mean(grouped, axis=-1, keepdims=True))
    spread = lax.optimization_barrier(jnp.mean(centred * centred, axis=-1, keepdims=True))
    return (centred * lax.rsqrt(spread + 1e-05)).reshape(full_shape) * gain + shift

def lstm_cell(gates, cells_prev, gain, shift):
    normed = group_norm(gates, gain, shift)
    quarter = normed.shape[-1] // 4
    input_gate = jax.nn.sigmoid(normed[..., :quarter])
    forget_gate = jax.nn.sigmoid(normed[..., quarter:2 * quarter])
    candidate = jnp.tanh(normed[..., 2 * quarter:3 * quarter])
    output_gate = jax.nn.sigmoid(normed[..., 3 * quarter:])
    cells_next = forget_gate * cells_prev + input_gate * candidate
    return (output_gate * jnp.tanh(cells_next), cells_next)

def forward(kernels, norm_params, end_params, head_bias, observed, targets, valid, count, hidden_init, cells_init):
    inputs_low = [low(end_params[0] * observed[:, frame_no, :, :, None] + end_params[1]) for frame_no in range(FRAMES)]
    margin = KERNEL // 2
    hidden_list = []
    cells_list = []
    outputs = []
    for layer_no in range(LAYERS):
        weight = low(kernels[layer_no]).reshape(KERNEL, KERNEL, IN_DIM, GATE_DIM)
        hidden_low = low(hidden_init[layer_no])
        cells = cells_init[layer_no]
        outputs = []
        outputs_low = []
        for frame_no in range(FRAMES):
            joined = jnp.concatenate([inputs_low[frame_no], hidden_low], axis=-1)
            conv = lax.conv_general_dilated(joined, weight, (1, 1), ((margin, margin), (margin, margin)), dimension_numbers=('NHWC', 'HWIO', 'NHWC'), precision=lax.Precision.HIGHEST)
            gates = low_back(conv)
            hidden, cells = lstm_cell(gates, cells, norm_params[0, layer_no], norm_params[1, layer_no])
            hidden_low = low(hidden)
            outputs.append(hidden)
            outputs_low.append(hidden_low)
        inputs_low = outputs_low
        hidden_list.append(hidden)
        cells_list.append(cells)
    total = jnp.zeros((), jnp.float32)
    for frame_no in range(FRAMES):
        predicted = lax.optimization_barrier(jnp.sum(outputs[frame_no] * end_params[2], axis=-1)) + head_bias[0]
        error = predicted - targets[:, frame_no]
        total = total + jnp.sum(valid[:, frame_no] * error * error)
    return (total / count, (jnp.stack(hidden_list), jnp.stack(cells_list)))

def adamw(weight, moment, second, grad, rate, correction):
    moment_new = 0.5 * moment + 0.5 * grad
    second_new = 0.5 * second + 0.5 * grad * grad
    update = moment_new / correction / (jnp.sqrt(second_new / correction) + 1e-08)
    return (weight - rate * (update + 0.01 * weight), moment_new, second_new)

def reference(observed, targets, pixel_mask, lengths, step_count, kernels, kernel_moment, kernel_second, norm_params, norm_moment, norm_second, end_params, end_moment, end_second, head_bias, head_moment, head_second, hidden_init, cells_init):
    frame_ids = jnp.arange(FRAMES, dtype=jnp.int32)
    counted = (frame_ids[None, :] < lengths[:, None]).astype(jnp.float32)
    valid = pixel_mask.astype(jnp.float32) * counted[:, :, None, None]
    count = jnp.maximum(jnp.sum(valid), 1.0)

    def objective(kern, norm_p, end_p, head_b):
        return forward(kern, norm_p, end_p, head_b, observed, targets, valid, count, hidden_init, cells_init)
    loss_value, pull, states = jax.vjp(objective, kernels, norm_params, end_params, head_bias, has_aux=True)
    grads = pull(jnp.ones((), jnp.float32))
    squares = jnp.zeros((), jnp.float32)
    for grad_part in grads:
        squares = squares + jnp.sum(grad_part * grad_part)
    grad_norm = jnp.sqrt(squares)
    factor = clip_limit / jnp.maximum(grad_norm, clip_limit)
    correction = 1.0 - jnp.power(0.5, step_count[0].astype(jnp.float32))
    kernel_rate = (KERNEL * KERNEL * IN_DIM) ** (-0.5)
    kern_out = adamw(kernels, kernel_moment, kernel_second, grads[0] * factor, kernel_rate, correction)
    norm_out = adamw(norm_params, norm_moment, norm_second, grads[1] * factor, small_rate, correction)
    end_out = adamw(end_params, end_moment, end_second, grads[2] * factor, small_rate, correction)
    head_out = adamw(head_bias, head_moment, head_second, grads[3] * factor, small_rate, correction)
    return (loss_value, grad_norm, kern_out[0], kern_out[1], kern_out[2], norm_out[0], norm_out[1], norm_out[2], end_out[0], end_out[1], end_out[2], head_out[0], head_out[1], head_out[2], states[0], states[1])
```

```python
import math

import jax
import jax.numpy as jnp
from jax import lax
from jax.experimental import pallas as pl
from jax.experimental.pallas import tpu as pltpu
from jax.sharding import PartitionSpec as P

IN_DIM = 512
KERNEL = 5
GROUP_SIZE = 64
MARGIN = KERNEL // 2
TAPS = KERNEL * KERNEL
ONES_ROW = 32

clip_limit = 0.005
small_rate = 0.1
BF = jnp.bfloat16
F32 = jnp.float32
I32 = jnp.int32
EXACT = lax.Precision.HIGHEST


def spread(x, axes):
    n = lax.axis_size(axes)
    return lax.all_to_all(jnp.broadcast_to(x[None], (n,) + x.shape), axes, 0, 0)


def shape(dims, kind):
    return jax.ShapeDtypeStruct(dims, kind)


def whole(array):
    dims = array.shape
    return pl.BlockSpec(dims, lambda *unused: (0,) * len(dims))


def columns_kernel(place, first, second, third, fourth, out):
    odd = place[1] == 1
    lower = lax.broadcasted_iota(I32, first.shape, 1) < GROUP_SIZE

    def pair(left, right):
        x, y = left[...], right[...]
        low = jnp.where(odd, pltpu.roll(x, GROUP_SIZE, 1), x)
        high = jnp.where(odd, y, pltpu.roll(y, GROUP_SIZE, 1))
        return jnp.where(lower, low, high).astype(BF)

    out[:, : 2 * GROUP_SIZE] = pair(first, second)
    out[:, 2 * GROUP_SIZE :] = pair(third, fourth)


def own_kernel_columns(kernels, block):
    own, gate_dim = kernels.shape
    lanes = 2 * GROUP_SIZE
    per_quarter = gate_dim // 4 // lanes
    step = own // 5
    place = jnp.stack([block // 2, block % 2]).astype(I32)

    def spec(quarter):
        return pl.BlockSpec((step, lanes), lambda i, where: (i, quarter * per_quarter + where[0]))

    return pl.pallas_call(
        columns_kernel,
        out_shape=shape((own, 4 * GROUP_SIZE), BF),
        grid_spec=pltpu.PrefetchScalarGridSpec(
            num_scalar_prefetch=1,
            grid=(5,),
            in_specs=[spec(q) for q in range(4)],
            out_specs=pl.BlockSpec((step, 4 * GROUP_SIZE), lambda i, where: (i, 0)),
        ),
        name="columns",
    )(place, kernels, kernels, kernels, kernels)


def group_mean(values):
    n = values.shape[1]
    same = (
        lax.broadcasted_iota(I32, (n, n), 0) // GROUP_SIZE
        == lax.broadcasted_iota(I32, (n, n), 1) // GROUP_SIZE
    )
    mixer = jnp.where(same, 1.0 / GROUP_SIZE, 0.0).astype(F32)
    return jnp.dot(values, mixer, precision=EXACT, preferred_element_type=F32)


def fill_bands(bands, image, columns):
    pixels = image.shape[0]
    edge = MARGIN * columns
    column = lax.broadcasted_iota(I32, image.shape, 0) % columns
    blank = jnp.zeros((edge, image.shape[1]), BF)
    for d in range(KERNEL):
        move = d - MARGIN
        moved = image if move == 0 else pltpu.roll(image, (-move) % pixels, 0)
        inside = (column + move >= 0) & (column + move < columns)
        bands[d, edge : edge + pixels, :] = jnp.where(inside, moved, 0.0).astype(BF)
        bands[d, :edge, :] = blank
        bands[d, edge + pixels :, :] = blank


def cell_parts(gates, cells_prev, gain, shift):
    width = cells_prev.shape[1]
    centred = gates - group_mean(gates)
    inverse = lax.rsqrt(group_mean(centred * centred) + 1e-05)
    norm = centred * inverse
    normed = norm * gain + shift
    input_gate = jax.nn.sigmoid(normed[:, :width])
    forget_gate = jax.nn.sigmoid(normed[:, width : 2 * width])
    candidate = jnp.tanh(normed[:, 2 * width : 3 * width])
    output_gate = jax.nn.sigmoid(normed[:, 3 * width :])
    cells = forget_gate * cells_prev + input_gate * candidate
    return norm, inverse, input_gate, forget_gate, candidate, output_gate, cells


def forward_kernel(
    columns, first_row, obs, hid, ends, weight, cells_prev, norms, head,
    gates_out, cells_out, hidden_out, low_out, turned_out, seen_out, bands, total,
):
    step = pl.program_id(0)
    pixels = total.shape[0]

    @pl.when(step == 0)
    def start():
        lifted = (ends[0:1, :] * obs[...] + ends[1:2, :]).astype(BF).astype(F32)
        fill_bands(bands, jnp.concatenate([lifted, hid[...].astype(F32)], axis=1), columns)
        total[...] = jnp.zeros_like(total)

    begin = pl.multiple_of((first_row[0] + step) * columns, columns)
    part = total[...]
    for d in range(KERNEL):
        part = part + jnp.dot(
            bands[d, pl.ds(begin, pixels), :], weight[d], preferred_element_type=F32
        )
    total[...] = part

    @pl.when(step == KERNEL - 1)
    def finish():
        gates = total[...]
        parts = cell_parts(gates, cells_prev[...], norms[0:1, :], norms[1:2, :])
        output_gate, cells = parts[5], parts[6]
        hidden = output_gate * jnp.tanh(cells)
        gates_out[...] = gates
        cells_out[...] = cells
        hidden_out[...] = hidden
        low_out[...] = hidden.astype(BF)
        turned_out[...] = jnp.transpose(hidden).astype(BF)
        seen_out[...] = lax.dot_general(
            head[...], hidden, (((1,), (1,)), ((), ())), precision=EXACT,
            preferred_element_type=F32,
        )


def forward_frame(columns, rows, first_row, obs, hid, ends, weight, cells_prev, norms, head):
    pixels, width = cells_prev.shape
    image = hid.shape[0]
    gate = 4 * width
    outs = (
        shape((pixels, gate), F32),
        shape((pixels, width), F32),
        shape((pixels, width), F32),
        shape((pixels, width), BF),
        shape((width, pixels), BF),
        shape((8, pixels), F32),
    )

    def body(*refs):
        forward_kernel(columns, *refs)

    return pl.pallas_call(
        body,
        out_shape=outs,
        grid_spec=pltpu.PrefetchScalarGridSpec(
            num_scalar_prefetch=1,
            grid=(KERNEL,),
            in_specs=[
                whole(obs),
                whole(hid),
                whole(ends),
                pl.BlockSpec((KERNEL, IN_DIM, gate), lambda i, first: (i, 0, 0)),
                whole(cells_prev),
                whole(norms),
                whole(head),
            ],
            out_specs=[whole(o) for o in outs],
            scratch_shapes=[
                pltpu.VMEM((KERNEL, image + 2 * MARGIN * columns, IN_DIM), BF),
                pltpu.VMEM((pixels, gate), F32),
            ],
        ),
        name="forward_frame",
    )(first_row, obs, hid, ends, weight, cells_prev, norms, head)


def backward_kernel(last, *refs):
    (scalars, seen, target, valid, gates, cells_prev, norms, head, looks) = refs[:9]
    grad_next, pieces = (None, ()) if last else (refs[9], refs[10:-6])
    low_out, cells_grad, sums_out, echo_out, rows_out, head_out = refs[-6:]
    pixels, width = cells_prev.shape
    gain = norms[0:1, :]
    error = jnp.sum(seen[...], axis=0, keepdims=True) + scalars[0] - target[...]
    weighted = valid[...] * error
    grad_row = 2.0 * weighted / scalars[1]
    rows_out[0:1, :] = grad_row
    rows_out[1:2, :] = weighted * error
    rows_out[2:8, :] = jnp.zeros((6, pixels), F32)
    grad_pred = jnp.transpose(jnp.broadcast_to(grad_row, (2 * GROUP_SIZE, pixels)))[:, :width]

    norm, inverse, input_gate, forget_gate, candidate, output_gate, cells = cell_parts(
        gates[...], cells_prev[...], gain, norms[1:2, :]
    )
    squashed = jnp.tanh(cells)
    grad_hidden = grad_pred * head[0:1, :]
    for piece in pieces:
        grad_hidden = grad_hidden + piece[...]
    head_out[...] = jnp.broadcast_to(
        jnp.sum(grad_pred * (output_gate * squashed), axis=0, keepdims=True), head_out.shape
    )
    grad_cells = grad_hidden * output_gate * (1.0 - squashed * squashed)
    if not last:
        grad_cells = grad_cells + grad_next[...]
    cells_grad[...] = grad_cells * forget_gate
    grad_normed = jnp.concatenate(
        [
            grad_cells * candidate * input_gate * (1.0 - input_gate),
            grad_cells * cells_prev[...] * forget_gate * (1.0 - forget_gate),
            grad_cells * input_gate * (1.0 - candidate * candidate),
            grad_hidden * squashed * output_gate * (1.0 - output_gate),
        ],
        axis=1,
    )
    sums_out[0:1, :] = jnp.sum(grad_normed * norm, axis=0, keepdims=True)
    sums_out[1:2, :] = jnp.sum(grad_normed, axis=0, keepdims=True)
    sums_out[2:8, :] = jnp.zeros((6, 4 * width), F32)
    scaled = grad_normed * gain
    grad_gates = inverse * (scaled - group_mean(scaled) - norm * group_mean(scaled * norm))
    low = grad_gates.astype(BF)
    low_out[...] = low
    echo_out[...] = jnp.dot(
        looks[...], low.astype(F32), precision=EXACT, preferred_element_type=F32
    )


def backward_frame(scalars, seen, target, valid, gates, cells_prev, norms, head, looks, later):
    pixels, width = cells_prev.shape
    gate = 4 * width
    outs = (
        shape((pixels, gate), BF),
        shape((pixels, width), F32),
        shape((8, gate), F32),
        shape((looks.shape[0], gate), F32),
        shape((8, pixels), F32),
        shape((8, width), F32),
    )
    args = [seen, target, valid, gates, cells_prev, norms, head, looks] + list(later)
    last = not later

    def body(*refs):
        backward_kernel(last, *refs)

    return pl.pallas_call(
        body,
        out_shape=outs,
        in_specs=[pl.BlockSpec(memory_space=pltpu.SMEM)] + [whole(a) for a in args],
        out_specs=[whole(o) for o in outs],
        grid=(1,),
        name="backward_cell",
    )(scalars, *args)


def hidden_kernel(columns, me, above, low, below, weight, *refs):
    outs, (bands, total, held) = refs[:-3], refs[-3:]
    step = pl.program_id(0)
    pixels = low.shape[0]
    blocks, unused, width = held.shape

    @pl.when(step == 0)
    def start():
        fill_bands(bands, low[...].astype(F32), columns)
        edge = MARGIN * columns
        if above is not None:
            for side, place in ((above, 0), (below, edge + pixels)):
                image = side[...].astype(F32)
                column = lax.broadcasted_iota(I32, image.shape, 0) % columns
                for d in range(KERNEL):
                    move = d - MARGIN
                    moved = image if move == 0 else pltpu.roll(image, (-move) % edge, 0)
                    inside = (column + move >= 0) & (column + move < columns)
                    bands[d, place : place + edge, :] = jnp.where(inside, moved, 0.0).astype(BF)
        total[...] = jnp.zeros_like(total)

    begin = pl.multiple_of((KERNEL - 1 - step) * columns, columns)
    part = total[...]
    for d in range(KERNEL):
        part = part + lax.dot_general(
            bands[KERNEL - 1 - d, pl.ds(begin, pixels), :],
            weight[d, 0],
            (((1,), (1,)), ((), ())),
            preferred_element_type=F32,
        )
    total[...] = part

    @pl.when(step == KERNEL - 1)
    def finish():
        for b in range(blocks):
            held[jnp.bitwise_xor(b, me[0])] = total[:, b * width : (b + 1) * width]
        for k in range(blocks):
            outs[k][...] = held[k]


def hidden_gradient(columns, blocks, me, sides, low, weight):
    pixels, gate = low.shape
    hidden_dim = weight.shape[1] // 2
    halves = weight.reshape(TAPS, 2, hidden_dim, gate)
    width = hidden_dim // blocks
    outs = (shape((pixels, width), F32),) * blocks
    args = [low] if sides is None else [sides[0], low, sides[1]]

    def body(me_ref, *refs):
        if sides is None:
            hidden_kernel(columns, me_ref, None, refs[0], None, *refs[1:])
        else:
            hidden_kernel(columns, me_ref, *refs)

    return pl.pallas_call(
        body,
        out_shape=outs,
        grid_spec=pltpu.PrefetchScalarGridSpec(
            num_scalar_prefetch=1,
            grid=(KERNEL,),
            in_specs=[whole(a) for a in args]
            + [pl.BlockSpec((KERNEL, 1, hidden_dim, gate), lambda i, where: (i, 1, 0, 0))],
            out_specs=[whole(o) for o in outs],
            scratch_shapes=[
                pltpu.VMEM((KERNEL, pixels + 2 * MARGIN * columns, gate), BF),
                pltpu.VMEM((pixels, hidden_dim), F32),
                pltpu.VMEM((blocks, pixels, width), F32),
            ],
        ),
        name="hidden_gradient",
    )(me, *args, halves)


def patches_kernel(columns, slabs, tiles, places, obs, ends, *refs):
    hid, (out, moves, patches, held) = refs[:tiles], refs[tiles:]
    own, image = out.shape
    span = moves.shape[0]
    for k in range(tiles):
        held[k] = hid[k][0]

    @pl.when(pl.program_id(0) == 0)
    def start():
        source = lax.broadcasted_iota(I32, (image, image), 0)
        target = lax.broadcasted_iota(I32, (image, image), 1)
        for k in range(span):
            row_off, col_off = places[2 + 2 * k], places[3 + 2 * k]
            column = target % columns + col_off
            hit = source == target + row_off * columns + col_off
            hit = hit & (column >= 0) & (column < columns)
            moves[k] = jnp.where(hit, 1.0, 0.0).astype(BF)

    lifted = (ends[:, 0:1] * obs[0] + ends[:, 1:2]).astype(BF)
    blocks = tiles // slabs
    parts = [lifted]
    for b in range(blocks):
        piece = [held[jnp.bitwise_xor(s * blocks + b, places[1])] for s in range(slabs)]
        parts.append(piece[0] if slabs == 1 else jnp.concatenate(piece, axis=1))
    joined = jnp.concatenate(parts, axis=0)
    for k in range(span):
        patches[k * IN_DIM : (k + 1) * IN_DIM, :] = jnp.dot(
            joined, moves[k], preferred_element_type=F32
        ).astype(BF)
    skip = pl.multiple_of(places[0], 16)
    out[...] = patches[pl.ds(skip, own), :]


def owned_patches(columns, slabs, own, span, places, obs, hid, width, row, ends):
    owners, unused, image = obs.shape
    tiles, pixels = len(hid), hid[0].shape[2]

    def body(*refs):
        patches_kernel(columns, slabs, tiles, *refs)

    return pl.pallas_call(
        body,
        out_shape=shape((own, owners * image), BF),
        grid_spec=pltpu.PrefetchScalarGridSpec(
            num_scalar_prefetch=1,
            grid=(owners,),
            in_specs=[
                pl.BlockSpec((1, 1, image), lambda s, where: (s, 0, 0)),
                whole(ends),
            ]
            + [pl.BlockSpec((1, width, pixels), lambda s, where: (s, row, 0))] * tiles,
            out_specs=pl.BlockSpec((own, image), lambda s, where: (0, s)),
            scratch_shapes=[
                pltpu.VMEM((span, image, image), BF),
                pltpu.VMEM((span * IN_DIM, image), BF),
                pltpu.VMEM((tiles, width, pixels), BF),
            ],
        ),
        name="owned_patches",
    )(places, obs, ends, *hid)


def adamw(weight, moment, second, grad, rate, correction):
    moment_new = 0.5 * moment + 0.5 * grad
    second_new = 0.5 * second + 0.5 * grad * grad
    update = moment_new / correction / (jnp.sqrt(second_new / correction) + 1e-08)
    return (weight - rate * (update + 0.01 * weight), moment_new, second_new)


def adamw_kernel(blocks, rate, me, scalars, *refs):
    grads = refs[:blocks]
    weight, moment, second, weight_out, moment_out, second_out, held = refs[blocks:]
    for k in range(blocks):
        held[k] = grads[k][...]
    width = held.shape[2] // 4
    placed = [held[jnp.bitwise_xor(b, me[0])] for b in range(blocks)]
    for q in range(4):
        grad = jnp.concatenate([p[:, q * width : (q + 1) * width] for p in placed], axis=1)
        cols = slice(q * blocks * width, (q + 1) * blocks * width)
        weight_out[:, cols], moment_out[:, cols], second_out[:, cols] = adamw(
            weight[:, cols], moment[:, cols], second[:, cols], grad * scalars[0], rate, scalars[1]
        )


def kernel_update(me, scalars, grads, weight, moment, second, rate):
    own, gate_dim = weight.shape
    blocks = len(grads)
    step = own // 10
    gate = gate_dim // blocks
    wide = pl.BlockSpec((step, gate_dim), lambda i, where: (i, 0))
    thin = pl.BlockSpec((step, gate), lambda i, where: (i, 0))

    def body(*refs):
        adamw_kernel(blocks, rate, *refs)

    return pl.pallas_call(
        body,
        out_shape=(shape((own, gate_dim), F32),) * 3,
        grid_spec=pltpu.PrefetchScalarGridSpec(
            num_scalar_prefetch=1,
            grid=(10,),
            in_specs=[pl.BlockSpec(memory_space=pltpu.SMEM)] + [thin] * blocks + [wide] * 3,
            out_specs=[wide] * 3,
            scratch_shapes=[pltpu.VMEM((blocks, step, gate), F32)],
        ),
        name="kernel_update",
    )(me, scalars, *grads, weight, moment, second)


def split_low(values):
    high = values.astype(BF)
    return high, (values - high.astype(F32)).astype(BF)


def per_device(
    observed,
    targets,
    pixel_mask,
    lengths,
    step_count,
    kernels,
    kernel_moment,
    kernel_second,
    norm_params,
    norm_moment,
    norm_second,
    end_params,
    end_moment,
    end_second,
    head_bias,
    head_moment,
    head_second,
    hidden_init,
    cells_init,
):
    tiles, owners = lax.axis_size("tile"), lax.axis_size("dp")
    streams, frames, tile_rows, columns = observed.shape
    height = tile_rows * tiles
    hidden_dim = end_params.shape[1]
    gate_dim = 4 * hidden_dim
    blocks = math.gcd(tiles, hidden_dim // GROUP_SIZE)
    slabs = tiles // blocks
    rows = height // slabs
    width = hidden_dim // blocks
    gate = 4 * width
    pixels, image = rows * columns, height * columns
    own = kernels.shape[1]
    assert streams == 1 and width == GROUP_SIZE and own % 80 == 0 and pixels == gate
    tile = lax.axis_index("tile")
    owner = lax.axis_index("dp")
    block, slab = tile % blocks, tile // blocks
    first_row = slab * rows
    groups = None
    if slabs > 1:
        groups = [[s * blocks + b for b in range(blocks)] for s in range(slabs)]

    weight = lax.all_gather(own_kernel_columns(kernels[0], block), "dp", axis=0, tiled=True)
    weight = weight.reshape(TAPS, IN_DIM, gate)

    frame_ids = lax.broadcasted_iota(I32, (1, frames), 1)
    counted = (frame_ids < lengths[:, None]).astype(F32)
    valid = pixel_mask.astype(F32) * counted[:, :, None, None]
    small = spread(jnp.stack([observed[0], targets[0], valid[0]]), ("dp", "tile"))
    small = small.reshape(owners, tiles, 3, frames, tile_rows * columns)
    small = small.transpose(2, 3, 0, 1, 4).reshape(3, frames, owners, image)
    count = jnp.maximum(jnp.sum(small[2]), 1.0)
    obs_all = small[0]
    mine = lax.dynamic_slice_in_dim(small, owner, 1, 2)
    mine_rows = lax.dynamic_slice_in_dim(mine, first_row * columns, pixels, 3)

    def own_columns(values):
        shaped = values.reshape(values.shape[:-1] + (4, hidden_dim))
        part = lax.dynamic_slice_in_dim(shaped, block * width, width, values.ndim)
        return part.reshape(values.shape[:-1] + (gate,))

    norms = own_columns(norm_params[:, 0])
    head = lax.dynamic_slice_in_dim(end_params[2], block * width, width, 0)
    head = jnp.broadcast_to(head[None], (8, width))
    ends = end_params[:2]
    ends_turned = ends.T

    me = jnp.reshape(block if slabs == 1 else jnp.zeros_like(block), (1,)).astype(I32)

    def all_tiles(values):
        if slabs > 1:
            got = lax.all_gather(values, "tile")
            return [got[k] for k in range(tiles)]
        held, order, stride = [values], [0], tiles // 2
        while stride:
            pairs = [(j, j ^ stride) for j in range(tiles)]
            held = held + [lax.ppermute(h, "tile", pairs) for h in held]
            order = order + [k ^ stride for k in order]
            stride //= 2
        return [held[order.index(k)] for k in range(tiles)]

    span = max((own * (i + 1) - 1) // IN_DIM - own * i // IN_DIM + 1 for i in range(owners))
    first_tap = jnp.minimum(owner * own // IN_DIM, TAPS - span)
    places = [owner * own - first_tap * IN_DIM, me[0]]
    for k in range(span):
        places += [(first_tap + k) // KERNEL - MARGIN, (first_tap + k) % KERNEL - MARGIN]
    places = jnp.stack(places).astype(I32)

    def patches_of(frame_no, hid, row):
        obs_rows = obs_all[frame_no].reshape(owners, 1, image)
        return owned_patches(
            columns, slabs, own, span, places, obs_rows, hid, width, row, ends_turned
        )

    states = jnp.stack([hidden_init[0, 0], cells_init[0, 0]])
    states = states.reshape(2, tile_rows * columns, blocks, width).transpose(2, 0, 1, 3)
    states = lax.all_to_all(states, "tile", 0, 0, axis_index_groups=groups)
    states = states.transpose(1, 0, 2, 3).reshape(2, pixels, width)
    low = states[0].astype(BF)
    cells = states[1]
    patches = [None] * frames
    patches[0] = patches_of(0, all_tiles(spread(low.T, "dp")), 0)

    def whole_hidden(values):
        got = lax.all_gather(values, "tile").reshape(slabs, blocks, pixels, width)
        return got.transpose(0, 2, 1, 3).reshape(image, hidden_dim)

    weight, patches[0] = lax.optimization_barrier((weight, patches[0]))
    first = jnp.reshape(first_row, (1,)).astype(I32)
    kept, turns, seen, turned = [], [], [], None
    for frame_no in range(frames):
        obs_column = mine[0, frame_no].reshape(image, 1)
        turns.append(turned)
        gates, cells_next, hidden, low_next, turned, seen_part = forward_frame(
            columns, rows, first, obs_column, whole_hidden(low), ends, weight, cells, norms, head
        )
        kept.append((gates, cells))
        cells, low = cells_next, low_next
        seen.append(seen_part[0])
    seen = lax.all_gather(jnp.stack(seen), "tile", axis_index_groups=groups)
    scalars = jnp.stack([head_bias[0], count])

    padded = jnp.pad(
        jnp.stack([mine[0, :, 0], jnp.ones_like(mine[0, :, 0])], axis=1).reshape(
            frames, 2, height, columns
        ),
        ((0, 0), (0, 0), (MARGIN, MARGIN), (MARGIN, MARGIN)),
    )
    padded = lax.dynamic_slice_in_dim(padded, first_row, rows + 2 * MARGIN, 2)
    looks = jnp.stack(
        [
            padded[:, :, a : a + rows, b : b + columns].reshape(frames, 2, pixels)
            for a in range(KERNEL)
            for b in range(KERNEL)
        ],
        axis=2,
    )
    looks = jnp.pad(looks, ((0, 0), (0, 0), (0, ONES_ROW - TAPS), (0, 0)))
    looks = looks.reshape(frames, 2 * ONES_ROW, pixels)

    sums = jnp.zeros((8, gate), F32)
    echo = jnp.zeros((2 * ONES_ROW, gate), F32)
    rows_sum = jnp.zeros((8, pixels), F32)
    head_sum = jnp.zeros((8, width), F32)
    later = ()
    parcels = [None] * frames
    for frame_no in reversed(range(frames)):
        gates, cells_prev = kept[frame_no]
        low, grad_cells, sums_part, echo_part, rows_part, head_part = backward_frame(
            scalars,
            seen[:, frame_no],
            mine_rows[1, frame_no],
            mine_rows[2, frame_no],
            gates,
            cells_prev,
            norms,
            head,
            looks[frame_no],
            later,
        )
        parcel = low if frame_no == 0 else jnp.concatenate([low, turns[frame_no]], axis=0)
        parcels[frame_no] = spread(parcel, "dp")
        sums, echo = sums + sums_part, echo + echo_part
        rows_sum, head_sum = rows_sum + rows_part, head_sum + head_part
        if frame_no > 0:
            sides = None
            if slabs > 1:
                edge = MARGIN * columns
                up = [(s, s - blocks) for s in range(blocks, tiles)]
                down = [(s - blocks, s) for s in range(blocks, tiles)]
                below = lax.ppermute(low[:edge], "tile", up)
                above = lax.ppermute(low[pixels - edge :], "tile", down)
                sides = (above, below)
            pieces = list(
                hidden_gradient(
                    columns, blocks, jnp.reshape(block, (1,)).astype(I32), sides, low, weight
                )
            )
            for k in range(1, blocks):
                pairs = [(j, j ^ k) for j in range(tiles)]
                pieces[k] = lax.ppermute(pieces[k], "tile", pairs)
            later = [grad_cells] + pieces

    hidden, cells, parcels[0] = lax.optimization_barrier((hidden, cells, parcels[0]))
    final = jnp.stack([hidden, cells]).reshape(2, blocks, tile_rows * columns, width)
    final = lax.all_to_all(final.transpose(1, 0, 2, 3), "tile", 0, 0, axis_index_groups=groups)
    final = final.transpose(1, 2, 0, 3).reshape(2, 1, 1, tile_rows, columns, hidden_dim)

    pieces = [None] * frames
    for frame_no in reversed(range(frames)):
        got = all_tiles(parcels[frame_no])
        if frame_no > 0:
            patches[frame_no] = patches_of(frame_no, got, pixels // width)
        pieces[frame_no] = [g[:, :pixels] for g in got]

    def block_gradient(k):
        grad = None
        for frame_no in reversed(range(frames)):
            if slabs == 1:
                piece = pieces[frame_no][k]
            else:
                piece = [pieces[frame_no][s * blocks + k] for s in range(slabs)]
                piece = jnp.stack(piece, axis=1)
            part = jnp.dot(
                patches[frame_no], piece.reshape(owners * image, gate), preferred_element_type=F32
            )
            grad = part if grad is None else grad + part
        return grad

    grads = [block_gradient(k) for k in range(blocks)]
    own_grad = grads[0]
    if slabs > 1:
        for b in range(1, blocks):
            own_grad = jnp.where(block == b, grads[b], own_grad)
    square = jnp.sum(own_grad * own_grad) * (slab == 0).astype(F32)

    lift_kernel = weight[:, :hidden_dim]
    echoes = echo.reshape(2, ONES_ROW, gate)[:, :TAPS]
    lift_grads = sum(
        jnp.einsum("ktg,tcg->kc", part, lift_kernel, preferred_element_type=F32)
        for part in split_low(echoes)
    )

    once = (block == 0).astype(F32)
    norm_part = jnp.zeros((2, 4, hidden_dim), F32)
    norm_part = lax.dynamic_update_slice_in_dim(
        norm_part, sums[:2].reshape(2, 4, width), block * width, 2
    )
    head_part = lax.dynamic_update_slice_in_dim(
        jnp.zeros((hidden_dim,), F32), head_sum[0], block * width, 0
    )
    packed = jnp.concatenate(
        [
            norm_part.reshape(-1),
            lift_grads.reshape(-1),
            head_part,
            jnp.sum(rows_sum[:2], axis=1) * once,
            jnp.reshape(square, (1,)),
        ]
    )
    total = jnp.sum(spread(packed, ("dp", "tile")), axis=0)
    grad_norms = total[: 2 * gate_dim].reshape(2, 1, gate_dim)
    grad_ends = total[2 * gate_dim : 2 * gate_dim + 3 * hidden_dim].reshape(3, hidden_dim)
    grad_head = total[-3:-2]
    loss_sum = total[-2]
    kernel_square = total[-1]

    squares = (
        kernel_square
        + jnp.sum(grad_norms * grad_norms)
        + jnp.sum(grad_ends * grad_ends)
        + jnp.sum(grad_head * grad_head)
    )
    grad_norm = jnp.sqrt(squares)
    factor = clip_limit / jnp.maximum(grad_norm, clip_limit)
    correction = 1.0 - jnp.power(0.5, step_count[0].astype(F32))
    kernel_rate = (TAPS * IN_DIM) ** (-0.5)
    kern_out = kernel_update(
        me,
        jnp.stack([factor, correction]),
        grads,
        kernels[0],
        kernel_moment[0],
        kernel_second[0],
        kernel_rate,
    )
    norm_out = adamw(
        norm_params, norm_moment, norm_second, grad_norms * factor, small_rate, correction
    )
    end_out = adamw(end_params, end_moment, end_second, grad_ends * factor, small_rate, correction)
    head_out = adamw(
        head_bias, head_moment, head_second, grad_head * factor, small_rate, correction
    )
    return (
        (loss_sum / count, grad_norm)
        + tuple(k[None] for k in kern_out)
        + norm_out
        + end_out
        + head_out
        + (final[0], final[1])
    )


def solution(mesh):
    rows = P("dp", None, "tile", None)
    kern = P(None, "dp", None)
    state = P(None, "dp", "tile", None, None)
    placed = (rows, rows, rows, P("dp"), P(), kern, kern, kern) + (P(),) * 9 + (state, state)
    outs = (P(), P(), kern, kern, kern) + (P(),) * 9 + (state, state)
    return jax.shard_map(
        per_device, mesh=mesh, in_specs=placed, out_specs=outs, check_vma=False
    )
```

```python
import math

import jax
import jax.numpy as jnp
from jax import lax
from jax.experimental import pallas as pl
from jax.experimental.pallas import tpu as pltpu
from jax.sharding import PartitionSpec as P

IN_DIM = 512
KERNEL = 5
GROUP_SIZE = 64
MARGIN = KERNEL // 2
TAPS = KERNEL * KERNEL
ONES_ROW = 32

clip_limit = 0.005
small_rate = 0.1
BF = jnp.bfloat16
F32 = jnp.float32
I32 = jnp.int32
EXACT = lax.Precision.HIGHEST


def spread(x, axes):
    n = lax.axis_size(axes)
    return lax.all_to_all(jnp.broadcast_to(x[None], (n,) + x.shape), axes, 0, 0)


def shape(dims, kind):
    return jax.ShapeDtypeStruct(dims, kind)


def hint(microseconds):
    return pl.CostEstimate(
        flops=int(microseconds * 0.35 * 1e9), bytes_accessed=int(microseconds * 0.35 * 3e6), transcendentals=0
    )


def whole(array):
    dims = array.shape
    return pl.BlockSpec(dims, lambda *unused: (0,) * len(dims))


def after(value, *others):
    def body(*refs):
        pass

    anywhere = pl.BlockSpec(memory_space=pl.ANY)
    return pl.pallas_call(
        body,
        out_shape=shape(value.shape, value.dtype),
        in_specs=[anywhere] * (1 + len(others)),
        out_specs=anywhere,
        input_output_aliases={0: 0},
        name="after",
    )(value, *others)


def columns_kernel(place, first, second, third, fourth, out):
    odd = place[1] == 1
    lower = lax.broadcasted_iota(I32, first.shape, 1) < GROUP_SIZE

    def pair(left, right):
        x, y = left[...], right[...]
        low = jnp.where(odd, pltpu.roll(x, GROUP_SIZE, 1), x)
        high = jnp.where(odd, y, pltpu.roll(y, GROUP_SIZE, 1))
        return jnp.where(lower, low, high).astype(BF)

    out[:, : 2 * GROUP_SIZE] = pair(first, second)
    out[:, 2 * GROUP_SIZE :] = pair(third, fourth)


def own_kernel_columns(kernels, block):
    own, gate_dim = kernels.shape
    lanes = 2 * GROUP_SIZE
    per_quarter = gate_dim // 4 // lanes
    steps = 2 if own % 32 == 0 else 5
    step = own // steps
    place = jnp.stack([block // 2, block % 2]).astype(I32)

    def spec(quarter):
        return pl.BlockSpec((step, lanes), lambda i, where: (i, quarter * per_quarter + where[0]))

    return pl.pallas_call(
        columns_kernel,
        out_shape=shape((own, 4 * GROUP_SIZE), BF),
        grid_spec=pltpu.PrefetchScalarGridSpec(
            num_scalar_prefetch=1,
            grid=(steps,),
            in_specs=[spec(q) for q in range(4)],
            out_specs=pl.BlockSpec((step, 4 * GROUP_SIZE), lambda i, where: (i, 0)),
        ),
        name="columns",
    )(place, kernels, kernels, kernels, kernels)


def group_mean(values):
    n = values.shape[1]
    same = (
        lax.broadcasted_iota(I32, (n, n), 0) // GROUP_SIZE
        == lax.broadcasted_iota(I32, (n, n), 1) // GROUP_SIZE
    )
    mixer = jnp.where(same, 1.0 / GROUP_SIZE, 0.0).astype(F32)
    return jnp.dot(values, mixer, precision=EXACT, preferred_element_type=F32)


def fill_bands(bands, image, columns, mirrored=False):
    pixels, depth = image.shape
    edge = MARGIN * columns
    column = lax.broadcasted_iota(I32, image.shape, 0) % columns
    blank = jnp.zeros((edge, depth), BF)
    for d in range(KERNEL):
        move = (MARGIN - d) if mirrored else (d - MARGIN)
        lanes = slice(d * depth, (d + 1) * depth)
        moved = image if move == 0 else pltpu.roll(image, (-move) % pixels, 0)
        inside = (column + move >= 0) & (column + move < columns)
        bands[edge : edge + pixels, lanes] = jnp.where(inside, moved, 0.0).astype(BF)
        bands[:edge, lanes] = blank
        bands[edge + pixels :, lanes] = blank


def cell_parts(gates, cells_prev, gain, shift):
    width = cells_prev.shape[1]
    centred = gates - group_mean(gates)
    inverse = lax.rsqrt(group_mean(centred * centred) + 1e-05)
    norm = centred * inverse
    normed = norm * gain + shift
    input_gate = jax.nn.sigmoid(normed[:, :width])
    forget_gate = jax.nn.sigmoid(normed[:, width : 2 * width])
    candidate = jnp.tanh(normed[:, 2 * width : 3 * width])
    output_gate = jax.nn.sigmoid(normed[:, 3 * width :])
    cells = forget_gate * cells_prev + input_gate * candidate
    return norm, inverse, input_gate, forget_gate, candidate, output_gate, cells


def forward_kernel(
    columns, first_row, obs, hid, ends, weight, cells_prev, norms, head,
    gates_out, cells_out, hidden_out, low_out, turned_out, seen_out, bands, total, near, arrived,
):
    pixels = total.shape[0]

    def fetch(step):
        return pltpu.make_async_copy(weight.at[step], near.at[step], arrived.at[step])

    for step in range(KERNEL):
        fetch(step).start()
    lifted = (ends[0:1, :] * obs[...] + ends[1:2, :]).astype(BF).astype(F32)
    fill_bands(bands, jnp.concatenate([lifted, hid[...].astype(F32)], axis=1), columns)
    total[...] = jnp.zeros_like(total)

    @pl.loop(0, KERNEL)
    def tap_row(step):
        begin = pl.multiple_of((first_row[0] + step) * columns, columns)
        fetch(step).wait()
        total[...] += jnp.dot(
            bands[pl.ds(begin, pixels), :], near[step], preferred_element_type=F32
        )

    gates = total[...]
    parts = cell_parts(gates, cells_prev[...], norms[0:1, :], norms[1:2, :])
    output_gate, cells = parts[5], parts[6]
    hidden = output_gate * jnp.tanh(cells)
    gates_out[...] = gates
    cells_out[...] = cells
    hidden_out[...] = hidden
    low_out[...] = hidden.astype(BF)
    turned_out[...] = jnp.broadcast_to(jnp.transpose(hidden).astype(BF)[None], turned_out.shape)
    seen_out[...] = lax.dot_general(
        head[...], hidden, (((1,), (1,)), ((), ())), precision=EXACT, preferred_element_type=F32
    )[0:1, :]


def forward_frame(copies, columns, first_row, obs, hid, ends, weight, cells_prev, norms, head):
    pixels, width = cells_prev.shape
    image = hid.shape[0]
    gate = 4 * width
    outs = (
        shape((pixels, gate), F32),
        shape((pixels, width), F32),
        shape((pixels, width), F32),
        shape((pixels, width), BF),
        shape((copies, width, pixels), BF),
        shape((1, pixels), F32),
    )

    def body(*refs):
        forward_kernel(columns, *refs)

    return pl.pallas_call(
        body,
        out_shape=outs,
        grid_spec=pltpu.PrefetchScalarGridSpec(
            num_scalar_prefetch=1,
            grid=(1,),
            in_specs=[
                whole(obs),
                whole(hid),
                whole(ends),
                pl.BlockSpec(memory_space=pl.ANY),
                whole(cells_prev),
                whole(norms),
                whole(head),
            ],
            out_specs=[whole(o) for o in outs],
            scratch_shapes=[
                pltpu.VMEM((image + 2 * MARGIN * columns, KERNEL * IN_DIM), BF),
                pltpu.VMEM((pixels, gate), F32),
                pltpu.VMEM((KERNEL, KERNEL * IN_DIM, gate), BF),
                pltpu.SemaphoreType.DMA((KERNEL,)),
            ],
        ),
        cost_estimate=hint(4),
        name="forward_frame",
    )(
        first_row, obs, hid, ends, weight.reshape(KERNEL, KERNEL * IN_DIM, gate), cells_prev,
        norms, head,
    )


def backward_kernel(last, *refs):
    (scalars, seen, target, valid, gates, cells_prev, norms, head, looks) = refs[:9]
    grad_next, pieces = (None, ()) if last else (refs[9], refs[10:-6])
    low_out, cells_grad, sums_out, echo_out, rows_out, head_out = refs[-6:]
    pixels, width = cells_prev.shape
    gain = norms[0:1, :]
    error = jnp.sum(seen[...], axis=0, keepdims=True) + scalars[0] - target[...]
    weighted = valid[...] * error
    grad_row = 2.0 * weighted / scalars[1]
    rows_out[0:1, :] = grad_row
    rows_out[1:2, :] = weighted * error
    rows_out[2:8, :] = jnp.zeros((6, pixels), F32)
    grad_pred = jnp.transpose(jnp.broadcast_to(grad_row, (2 * GROUP_SIZE, pixels)))[:, :width]

    norm, inverse, input_gate, forget_gate, candidate, output_gate, cells = cell_parts(
        gates[...], cells_prev[...], gain, norms[1:2, :]
    )
    squashed = jnp.tanh(cells)
    grad_hidden = grad_pred * head[0:1, :]
    for piece in pieces:
        grad_hidden = grad_hidden + piece[...]
    head_out[...] = jnp.broadcast_to(
        jnp.sum(grad_pred * (output_gate * squashed), axis=0, keepdims=True), head_out.shape
    )
    grad_cells = grad_hidden * output_gate * (1.0 - squashed * squashed)
    if not last:
        grad_cells = grad_cells + grad_next[...]
    cells_grad[...] = grad_cells * forget_gate
    grad_normed = jnp.concatenate(
        [
            grad_cells * candidate * input_gate * (1.0 - input_gate),
            grad_cells * cells_prev[...] * forget_gate * (1.0 - forget_gate),
            grad_cells * input_gate * (1.0 - candidate * candidate),
            grad_hidden * squashed * output_gate * (1.0 - output_gate),
        ],
        axis=1,
    )
    sums_out[0:1, :] = jnp.sum(grad_normed * norm, axis=0, keepdims=True)
    sums_out[1:2, :] = jnp.sum(grad_normed, axis=0, keepdims=True)
    sums_out[2:8, :] = jnp.zeros((6, 4 * width), F32)
    scaled = grad_normed * gain
    grad_gates = inverse * (scaled - group_mean(scaled) - norm * group_mean(scaled * norm))
    low = grad_gates.astype(BF)
    low_out[...] = jnp.broadcast_to(low[None], low_out.shape)
    echo_out[...] = jnp.dot(
        looks[...], low.astype(F32), precision=EXACT, preferred_element_type=F32
    )


def backward_frame(
    copies, scalars, seen, target, valid, gates, cells_prev, norms, head, looks, later
):
    pixels, width = cells_prev.shape
    gate = 4 * width
    outs = (
        shape((copies, pixels, gate), BF),
        shape((pixels, width), F32),
        shape((8, gate), F32),
        shape((looks.shape[0], gate), F32),
        shape((8, pixels), F32),
        shape((8, width), F32),
    )
    args = [seen, target, valid, gates, cells_prev, norms, head, looks] + list(later)
    last = not later

    def body(*refs):
        backward_kernel(last, *refs)

    return pl.pallas_call(
        body,
        out_shape=outs,
        in_specs=[pl.BlockSpec(memory_space=pltpu.SMEM)] + [whole(a) for a in args],
        out_specs=[whole(o) for o in outs],
        grid=(1,),
        cost_estimate=hint(4),
        name="backward_cell",
    )(scalars, *args)


def hidden_kernel(columns, me, above, low, below, weight, *refs):
    outs, (bands, total, held, near, arrived) = refs[:-5], refs[-5:]
    pixels = low.shape[1]
    blocks, unused, width = held.shape

    def fetch(step):
        return pltpu.make_async_copy(
            weight.at[pl.ds(step * KERNEL, KERNEL), 1], near.at[step], arrived.at[step]
        )

    for step in range(KERNEL):
        fetch(step).start()
    fill_bands(bands, low[0].astype(F32), columns, mirrored=True)
    edge = MARGIN * columns
    if above is not None:
        for side, place in ((above, 0), (below, edge + pixels)):
            image = side[...].astype(F32)
            column = lax.broadcasted_iota(I32, image.shape, 0) % columns
            depth = image.shape[1]
            for d in range(KERNEL):
                move = MARGIN - d
                moved = image if move == 0 else pltpu.roll(image, (-move) % edge, 0)
                inside = (column + move >= 0) & (column + move < columns)
                bands[place : place + edge, d * depth : (d + 1) * depth] = jnp.where(
                    inside, moved, 0.0
                ).astype(BF)
    total[...] = jnp.zeros_like(total)

    @pl.loop(0, KERNEL)
    def tap_row(step):
        begin = pl.multiple_of((KERNEL - 1 - step) * columns, columns)
        fetch(step).wait()
        taps = jnp.concatenate([near[step, d] for d in range(KERNEL)], axis=1)
        total[...] += lax.dot_general(
            bands[pl.ds(begin, pixels), :],
            taps,
            (((1,), (1,)), ((), ())),
            preferred_element_type=F32,
        )

    for b in range(blocks):
        held[jnp.bitwise_xor(b, me[0])] = total[:, b * width : (b + 1) * width]
    for k in range(blocks):
        outs[k][...] = held[k]


def hidden_gradient(columns, blocks, me, sides, low, weight):
    unused, pixels, gate = low.shape
    hidden_dim = weight.shape[1] // 2
    halves = weight.reshape(TAPS, 2, hidden_dim, gate)
    width = hidden_dim // blocks
    outs = (shape((pixels, width), F32),) * blocks
    args = [low] if sides is None else [sides[0], low, sides[1]]
    specs = [pl.BlockSpec((1,) + a.shape[1:], lambda *i: (0, 0, 0)) if a is low else whole(a) for a in args]

    def body(me_ref, *refs):
        if sides is None:
            hidden_kernel(columns, me_ref, None, refs[0], None, *refs[1:])
        else:
            hidden_kernel(columns, me_ref, *refs)

    return pl.pallas_call(
        body,
        out_shape=outs,
        grid_spec=pltpu.PrefetchScalarGridSpec(
            num_scalar_prefetch=1,
            grid=(1,),
            in_specs=specs + [pl.BlockSpec(memory_space=pl.ANY)],
            out_specs=[whole(o) for o in outs],
            scratch_shapes=[
                pltpu.VMEM((pixels + 2 * MARGIN * columns, KERNEL * gate), BF),
                pltpu.VMEM((pixels, hidden_dim), F32),
                pltpu.VMEM((blocks, pixels, width), F32),
                pltpu.VMEM((KERNEL, KERNEL, hidden_dim, gate), BF),
                pltpu.SemaphoreType.DMA((KERNEL,)),
            ],
        ),
        cost_estimate=hint(4),
        name="hidden_gradient",
    )(me, *args, halves)


def patches_kernel(columns, slabs, tiles, places, obs, ends, *refs):
    hid, (out, moves, patches, held) = refs[:tiles], refs[tiles:]
    own, image = out.shape
    span = moves.shape[0]
    for k in range(tiles):
        held[k] = hid[k][0]

    @pl.when(pl.program_id(0) == 0)
    def start():
        source = lax.broadcasted_iota(I32, (image, image), 0)
        target = lax.broadcasted_iota(I32, (image, image), 1)
        for k in range(span):
            row_off, col_off = places[2 + 2 * k], places[3 + 2 * k]
            column = target % columns + col_off
            hit = source == target + row_off * columns + col_off
            hit = hit & (column >= 0) & (column < columns)
            moves[k] = jnp.where(hit, 1.0, 0.0).astype(BF)

    lifted = (ends[:, 0:1] * obs[0] + ends[:, 1:2]).astype(BF)
    blocks = tiles // slabs
    parts = [lifted]
    for b in range(blocks):
        piece = [held[jnp.bitwise_xor(s * blocks + b, places[1])] for s in range(slabs)]
        parts.append(piece[0] if slabs == 1 else jnp.concatenate(piece, axis=1))
    joined = jnp.concatenate(parts, axis=0)
    for k in range(span):
        patches[k * IN_DIM : (k + 1) * IN_DIM, :] = jnp.dot(
            joined, moves[k], preferred_element_type=F32
        ).astype(BF)
    skip = pl.multiple_of(places[0], 16)
    out[...] = patches[pl.ds(skip, own), :]


def owned_patches(columns, slabs, own, span, places, obs, hid, ends):
    owners, unused, image = obs.shape
    tiles, (unused_too, width, pixels) = len(hid), hid[0].shape

    def body(*refs):
        patches_kernel(columns, slabs, tiles, *refs)

    return pl.pallas_call(
        body,
        out_shape=shape((own, owners * image), BF),
        grid_spec=pltpu.PrefetchScalarGridSpec(
            num_scalar_prefetch=1,
            grid=(owners,),
            in_specs=[
                pl.BlockSpec((1, 1, image), lambda s, where: (s, 0, 0)),
                whole(ends),
            ]
            + [pl.BlockSpec((1, width, pixels), lambda s, where: (s, 0, 0))] * tiles,
            out_specs=pl.BlockSpec((own, image), lambda s, where: (0, s)),
            scratch_shapes=[
                pltpu.VMEM((span, image, image), BF),
                pltpu.VMEM((span * IN_DIM, image), BF),
                pltpu.VMEM((tiles, width, pixels), BF),
            ],
        ),
        cost_estimate=hint(9),
        name="owned_patches",
    )(places, obs, ends, *hid)


def adamw(weight, moment, second, grad, rate, correction):
    moment_new = 0.5 * moment + 0.5 * grad
    second_new = 0.5 * second + 0.5 * grad * grad
    update = moment_new / correction / (jnp.sqrt(second_new / correction) + 1e-08)
    return (weight - rate * (update + 0.01 * weight), moment_new, second_new)


def rows_at_once(own):
    return 16 * math.gcd(own // 16, 20)


def patch_dot(patch, pieces):
    flat = [p[...].reshape(patch.shape[1], p.shape[2]) for p in pieces]
    signal = flat[0] if len(flat) == 1 else jnp.concatenate(flat, axis=1)
    return jnp.dot(patch[...], signal, preferred_element_type=F32)


def gradient_kernel(blocks, squared, patch, *refs):
    pieces, refs = refs[:blocks], refs[blocks:]
    grad = patch_dot(patch, pieces)
    gate = pieces[0].shape[2]
    if squared:
        base, grad_out, square_out = refs
        grad = grad + base[...]

        @pl.when(pl.program_id(0) == 0)
        def start():
            square_out[...] = jnp.zeros_like(square_out)

        lanes = square_out.shape[1]
        square = grad * grad
        square = square[:, :lanes] + square[:, lanes:]
        square_out[...] += jnp.sum(square, axis=0, keepdims=True)
        grad_out[...] = grad
    else:
        for k in range(blocks):
            refs[k][...] = grad[:, k * gate : (k + 1) * gate]


def patch_gradient(patch, pieces, base=None, waits=()):
    own, gate = patch.shape[0], pieces[0].shape[2]
    step = own // 2
    rows = pl.BlockSpec((step, gate), lambda i: (i, 0))
    outs = [shape((own, gate), F32) for p in pieces]
    out_specs = [rows] * len(pieces)
    args = [patch] + list(pieces)
    in_specs = [pl.BlockSpec((step, patch.shape[1]), lambda i: (i, 0))] + [whole(p) for p in pieces]
    if base is not None:
        args, in_specs = args + [base], in_specs + [rows]
        outs = outs + [shape((1, gate // 2), F32)]
        out_specs = out_specs + [pl.BlockSpec((1, gate // 2), lambda i: (0, 0))]

    n = len(args)
    args, in_specs = args + list(waits), in_specs + [pl.BlockSpec(memory_space=pl.ANY)] * len(waits)

    def body(*refs):
        gradient_kernel(len(pieces), base is not None, *refs[:n], *refs[n + len(waits) :])

    return pl.pallas_call(
        body,
        out_shape=tuple(outs),
        grid=(own // step,),
        in_specs=in_specs,
        out_specs=out_specs,
        compiler_params=pltpu.CompilerParams(vmem_limit_bytes=60 << 20),
        cost_estimate=hint(3 + 2 * len(pieces)),
        name="patch_gradient",
    )(*args)


def small_update(scalars, everyone, triples, factor_row, smalls_out, measures_out):
    total = jnp.sum(everyone[...], axis=0)
    lanes = total.shape[1]
    gate_dim, hidden_dim = triples[0].shape[2], triples[3].shape[1]
    norm_rows = 2 * gate_dim // lanes
    end_rows = 3 * hidden_dim // lanes
    last = norm_rows + end_rows
    row = lax.broadcasted_iota(I32, total.shape, 0)
    lane = lax.broadcasted_iota(I32, total.shape, 1)
    wide = (row < last) | ((row == last) & (lane == 0))
    alone = row == last + 1
    squares = jnp.where(wide, total * total, jnp.where(alone, total, 0.0))
    grad_norm = jnp.sqrt(jnp.sum(jnp.sum(squares, axis=0, keepdims=True), axis=1, keepdims=True))
    factor = clip_limit / jnp.maximum(grad_norm, clip_limit)
    factor_row[...] = jnp.broadcast_to(factor, factor_row.shape)
    measures_out[0][...] = total[last : last + 1, 1:2] / scalars[1]
    measures_out[1][...] = grad_norm

    def line(begin, length):
        return jnp.concatenate([total[r : r + 1, :] for r in range(begin, begin + length)], axis=1)

    def update(place, grad, index):
        found = [t[index] for t in triples[place : place + 3]]
        got = adamw(*found, grad * factor, small_rate, scalars[0])
        for out, value in zip(smalls_out[place : place + 3], got):
            out[index] = value

    for r in range(2):
        update(0, line(r * norm_rows // 2, norm_rows // 2), r)
    for r in range(3):
        update(3, line(norm_rows + r * end_rows // 3, end_rows // 3), slice(r, r + 1))
    update(6, total[last : last + 1, 0:1], slice(0, 1))


def last_kernel(blocks, extra, rate, me, scalars, everyone, *refs):
    triples, refs = refs[:9], refs[9:]
    bases, refs = refs[:blocks], refs[blocks:]
    pieces, refs = refs[:extra], refs[extra:]
    held, factor_row = refs[-2:]
    weight, moment, second, weight_out, moment_out, second_out = refs[:6]
    measures_out, smalls_out = refs[6:8], refs[8:17]

    @pl.when(pl.program_id(0) == 0)
    def start():
        small_update(scalars, everyone, triples, factor_row, smalls_out, measures_out)

    for k in range(blocks):
        held[k] = bases[k][...]
    if extra:
        patch, pieces = pieces[0], pieces[1:]
        grad = patch_dot(patch, pieces)
        gate = held.shape[2]
        for k in range(1, blocks):
            held[k] += grad[:, (k - 1) * gate : k * gate]
    width = held.shape[2] // 4
    placed = [held[jnp.bitwise_xor(b, me[0])] for b in range(blocks)]
    for q in range(4):
        grad = jnp.concatenate([p[:, q * width : (q + 1) * width] for p in placed], axis=1)
        cols = slice(q * blocks * width, (q + 1) * blocks * width)
        weight_out[:, cols], moment_out[:, cols], second_out[:, cols] = adamw(
            weight[:, cols], moment[:, cols], second[:, cols], grad * factor_row[...], rate,
            scalars[0],
        )


def last_update(me, scalars, everyone, smalls, bases, late, kernel_triple, rate):
    own, gate_dim = kernel_triple[0].shape
    blocks = len(bases)
    step = rows_at_once(own)
    gate = gate_dim // blocks
    wide = pl.BlockSpec((step, gate_dim), lambda i, where: (i, 0))
    thin = pl.BlockSpec((step, gate), lambda i, where: (i, 0))
    late_specs = []
    if late:
        late_specs = [pl.BlockSpec((step, late[0].shape[1]), lambda i, where: (i, 0))]
        late_specs += [whole(p) for p in late[1:]]
    measures = [shape((1, 1), F32)] * 2

    def body(*refs):
        n = 3 + 9 + blocks + len(late)
        ins, outs = refs[: n + 3], refs[n + 3 :]
        last_kernel(blocks, len(late), rate, *ins, *outs)

    return pl.pallas_call(
        body,
        out_shape=tuple([shape((own, gate_dim), F32)] * 3 + measures + [shape(t.shape, F32) for t in smalls]),
        grid_spec=pltpu.PrefetchScalarGridSpec(
            num_scalar_prefetch=1,
            grid=(own // step,),
            in_specs=[pl.BlockSpec(memory_space=pltpu.SMEM), whole(everyone)]
            + [whole(t) for t in smalls]
            + [thin] * blocks
            + late_specs
            + [wide] * 3,
            out_specs=[wide] * 3 + [whole(m) for m in measures] + [whole(t) for t in smalls],
            scratch_shapes=[
                pltpu.VMEM((blocks, step, gate), F32),
                pltpu.VMEM((1, gate_dim // 4), F32),
            ],
        ),
        compiler_params=pltpu.CompilerParams(vmem_limit_bytes=60 << 20),
        cost_estimate=hint(22),
        name="last_update",
    )(me, scalars, everyone, *smalls, *bases, *late, *kernel_triple)


def split_low(values):
    high = values.astype(BF)
    return high, (values - high.astype(F32)).astype(BF)


def per_device(
    observed,
    targets,
    pixel_mask,
    lengths,
    step_count,
    kernels,
    kernel_moment,
    kernel_second,
    norm_params,
    norm_moment,
    norm_second,
    end_params,
    end_moment,
    end_second,
    head_bias,
    head_moment,
    head_second,
    hidden_init,
    cells_init,
):
    tiles, owners = lax.axis_size("tile"), lax.axis_size("dp")
    streams, frames, tile_rows, columns = observed.shape
    height = tile_rows * tiles
    hidden_dim = end_params.shape[1]
    gate_dim = 4 * hidden_dim
    blocks = math.gcd(tiles, hidden_dim // GROUP_SIZE)
    slabs = tiles // blocks
    rows = height // slabs
    width = hidden_dim // blocks
    gate = 4 * width
    pixels, image = rows * columns, height * columns
    own = kernels.shape[1]
    assert streams == 1 and width == GROUP_SIZE and own % 80 == 0 and pixels == gate
    tile = lax.axis_index("tile")
    owner = lax.axis_index("dp")
    block, slab = tile % blocks, tile // blocks
    first_row = slab * rows
    groups = None
    if slabs > 1:
        groups = [[s * blocks + b for b in range(blocks)] for s in range(slabs)]

    weight = lax.all_gather(own_kernel_columns(kernels[0], block), "dp", axis=0, tiled=True)
    weight = weight.reshape(TAPS, IN_DIM, gate)

    frame_ids = lax.broadcasted_iota(I32, (1, frames), 1)
    counted = (frame_ids < lengths[:, None]).astype(F32)
    valid = pixel_mask.astype(F32) * counted[:, :, None, None]
    small = spread(jnp.stack([observed[0], targets[0], valid[0]]), ("dp", "tile"))
    small = small.reshape(owners, tiles, 3, frames, tile_rows * columns)
    small = small.transpose(2, 3, 0, 1, 4).reshape(3, frames, owners, image)
    count = jnp.maximum(jnp.sum(small[2]), 1.0)
    obs_all = small[0]
    mine = lax.dynamic_slice_in_dim(small, owner, 1, 2)
    mine_rows = lax.dynamic_slice_in_dim(mine, first_row * columns, pixels, 3)

    def own_columns(values):
        shaped = values.reshape(values.shape[:-1] + (4, hidden_dim))
        part = lax.dynamic_slice_in_dim(shaped, block * width, width, values.ndim)
        return part.reshape(values.shape[:-1] + (gate,))

    norms = own_columns(norm_params[:, 0])
    head = lax.dynamic_slice_in_dim(end_params[2], block * width, width, 0)
    head = jnp.broadcast_to(head[None], (8, width))
    ends = end_params[:2]
    ends_turned = ends.T

    me = jnp.reshape(block if slabs == 1 else jnp.zeros_like(block), (1,)).astype(I32)

    def all_tiles(values, between=()):
        if slabs > 1:
            got = lax.all_gather(values, "tile")
            return [got[k] for k in range(tiles)]
        held, order, stride = [values], [0], tiles // 2
        while stride:
            pairs = [(j, j ^ stride) for j in range(tiles)]
            held = held + [lax.ppermute(h, "tile", pairs) for h in held]
            if between and stride > 1:
                held[1:] = [after(h, *between) for h in held[1:]]
            order = order + [k ^ stride for k in order]
            stride //= 2
        return [held[order.index(k)] for k in range(tiles)]

    span = max((own * (i + 1) - 1) // IN_DIM - own * i // IN_DIM + 1 for i in range(owners))
    first_tap = jnp.minimum(owner * own // IN_DIM, TAPS - span)
    places = [owner * own - first_tap * IN_DIM, me[0]]
    for k in range(span):
        places += [(first_tap + k) // KERNEL - MARGIN, (first_tap + k) % KERNEL - MARGIN]
    places = jnp.stack(places).astype(I32)

    def patches_of(frame_no, hid):
        obs_rows = obs_all[frame_no].reshape(owners, 1, image)
        return owned_patches(columns, slabs, own, span, places, obs_rows, hid, ends_turned)

    states = jnp.stack([hidden_init[0, 0], cells_init[0, 0]])
    states = states.reshape(2, tile_rows * columns, blocks, width).transpose(2, 0, 1, 3)
    states = lax.all_to_all(states, "tile", 0, 0, axis_index_groups=groups)
    states = states.transpose(1, 0, 2, 3).reshape(2, pixels, width)
    low = states[0].astype(BF)
    cells = states[1]
    patches = [None] * frames
    patches[0] = patches_of(0, all_tiles(spread(low.T, "dp")))

    def whole_hidden(values):
        got = lax.all_gather(values, "tile").reshape(slabs, blocks, pixels, width)
        return got.transpose(0, 2, 1, 3).reshape(image, hidden_dim)

    weight, patches[0] = lax.optimization_barrier((weight, patches[0]))
    first = jnp.reshape(first_row, (1,)).astype(I32)
    kept, seen, turns = [], [], [None] * frames
    for frame_no in range(frames):
        obs_column = mine[0, frame_no].reshape(image, 1)
        gates, cells_next, hidden, low_next, turned, seen_part = forward_frame(
            owners, columns, first, obs_column, whole_hidden(low), ends, weight, cells, norms, head
        )
        kept.append((gates, cells))
        cells, low = cells_next, low_next
        seen.append(seen_part[0])
        if frame_no + 1 < frames:
            turns[frame_no + 1] = lax.all_to_all(turned, "dp", 0, 0)
    seen = lax.all_gather(jnp.stack(seen), "tile", axis_index_groups=groups)
    seen, turns[1:] = lax.optimization_barrier((seen, turns[1:]))
    turns[1:] = [all_tiles(t) for t in turns[1:]]
    scalars = jnp.stack([head_bias[0], count])

    padded = jnp.pad(
        jnp.stack([mine[0, :, 0], jnp.ones_like(mine[0, :, 0])], axis=1).reshape(
            frames, 2, height, columns
        ),
        ((0, 0), (0, 0), (MARGIN, MARGIN), (MARGIN, MARGIN)),
    )
    padded = lax.dynamic_slice_in_dim(padded, first_row, rows + 2 * MARGIN, 2)
    looks = jnp.stack(
        [
            padded[:, :, a : a + rows, b : b + columns].reshape(frames, 2, pixels)
            for a in range(KERNEL)
            for b in range(KERNEL)
        ],
        axis=2,
    )
    looks = jnp.pad(looks, ((0, 0), (0, 0), (0, ONES_ROW - TAPS), (0, 0)))
    looks = looks.reshape(frames, 2 * ONES_ROW, pixels)

    sums = jnp.zeros((8, gate), F32)
    echo = jnp.zeros((2 * ONES_ROW, gate), F32)
    rows_sum = jnp.zeros((8, pixels), F32)
    head_sum = jnp.zeros((8, width), F32)
    later = ()
    parcels = [None] * frames
    for frame_no in reversed(range(frames)):
        gates, cells_prev = kept[frame_no]
        lows, grad_cells, sums_part, echo_part, rows_part, head_part = backward_frame(
            owners,
            scalars,
            seen[:, frame_no],
            mine_rows[1, frame_no],
            mine_rows[2, frame_no],
            gates,
            cells_prev,
            norms,
            head,
            looks[frame_no],
            later,
        )
        parcels[frame_no] = lax.all_to_all(lows, "dp", 0, 0)
        sums, echo = sums + sums_part, echo + echo_part
        rows_sum, head_sum = rows_sum + rows_part, head_sum + head_part
        if frame_no > 0:
            sides = None
            if slabs > 1:
                edge = MARGIN * columns
                up = [(s, s - blocks) for s in range(blocks, tiles)]
                down = [(s - blocks, s) for s in range(blocks, tiles)]
                below = lax.ppermute(lows[0, :edge], "tile", up)
                above = lax.ppermute(lows[0, pixels - edge :], "tile", down)
                sides = (above, below)
            pieces = list(
                hidden_gradient(
                    columns, blocks, jnp.reshape(block, (1,)).astype(I32), sides, lows, weight
                )
            )
            for k in range(1, blocks):
                pairs = [(j, j ^ k) for j in range(tiles)]
                pieces[k] = lax.ppermute(pieces[k], "tile", pairs)
            patches[frame_no] = patches_of(frame_no, turns[frame_no])
            later = [grad_cells] + pieces

    own_grad = jnp.zeros((8, gate), F32)
    if slabs == 1:
        for frame_no in reversed(range(1, frames)):
            part = patch_gradient(patches[frame_no], [parcels[frame_no]])[0]
            own_grad = part if frame_no == frames - 1 else own_grad + part
    echo = after(echo, own_grad)
    lift_kernel = weight[:, :hidden_dim]
    echoes = echo.reshape(2, ONES_ROW, gate)[:, :TAPS]
    lift_grads = sum(
        jnp.einsum("ktg,tcg->kc", part, lift_kernel, preferred_element_type=F32)
        for part in split_low(echoes)
    )

    pieces = [None] + [all_tiles(p, [own_grad, lift_grads]) for p in parcels[1:]]

    states = after(jnp.stack([hidden, cells]), own_grad)
    states = states.reshape(2, blocks, tile_rows * columns, width)
    final = []
    for k in range(blocks):
        part = lax.dynamic_slice_in_dim(states, jnp.bitwise_xor(block, k), 1, 1)
        if k:
            part = lax.ppermute(part, "tile", [(j, j ^ k) for j in range(tiles)])
        final.append(part)
    final = jnp.concatenate(final, axis=1)
    final = jnp.take(final, jnp.bitwise_xor(jnp.arange(blocks), block), axis=1)
    final = final.transpose(0, 2, 1, 3).reshape(2, 1, 1, tile_rows, columns, hidden_dim)
    once = (block == 0).astype(F32)
    norm_part = jnp.zeros((2, 4, hidden_dim), F32)
    norm_part = lax.dynamic_update_slice_in_dim(
        norm_part, sums[:2].reshape(2, 4, width), block * width, 2
    )
    head_part = lax.dynamic_update_slice_in_dim(
        jnp.zeros((hidden_dim,), F32), head_sum[0], block * width, 0
    )
    packed = jnp.concatenate(
        [
            norm_part.reshape(-1),
            lift_grads.reshape(-1),
            head_part,
            jnp.sum(rows_sum[:2], axis=1) * once,
        ]
    )
    lanes = 2 * GROUP_SIZE
    packed = jnp.pad(packed, (0, -packed.shape[0] % lanes)).reshape(-1, lanes)
    devices = owners * tiles
    if slabs == 1:
        own_grad, square = patch_gradient(patches[0], [parcels[0]], own_grad, waits=[final])
        packed = jnp.broadcast_to(jnp.concatenate([packed, square])[None], (devices, packed.shape[0] + 1, lanes))
        bases = [0.0] * (blocks - 1)
        for frame_no in reversed(range(1, frames)):
            got = patch_gradient(patches[frame_no], pieces[frame_no][1:], waits=[packed])
            bases = [b + g for b, g in zip(bases, got)]
        everyone = lax.all_to_all(packed, ("dp", "tile"), 0, 0)
        pieces[0] = all_tiles(parcels[0], [everyone] + bases)
        bases, late = [own_grad] + bases, [patches[0]] + pieces[0][1:]
    else:
        pieces[0] = all_tiles(parcels[0])
        bases, late = [], []
        for b in range(blocks):
            grad = 0.0
            for frame_no in range(frames):
                piece = [pieces[frame_no][s * blocks + b] for s in range(slabs)]
                piece = jnp.stack(piece, axis=1).reshape(owners * image, gate)
                grad = grad + jnp.dot(patches[frame_no], piece, preferred_element_type=F32)
            bases.append(grad)
        own_grad = bases[0]
        for b in range(1, blocks):
            own_grad = jnp.where(block == b, bases[b], own_grad)
        square = jnp.sum(own_grad * own_grad, axis=0, keepdims=True) * (slab == 0).astype(F32)
        square = square[:, : 2 * GROUP_SIZE] + square[:, 2 * GROUP_SIZE :]
        packed = jnp.broadcast_to(jnp.concatenate([packed, square])[None], (devices, packed.shape[0] + 1, lanes))
        everyone = lax.all_to_all(packed, ("dp", "tile"), 0, 0)
    correction = 1.0 - jnp.power(0.5, step_count[0].astype(F32))
    kernel_rate = (TAPS * IN_DIM) ** (-0.5)
    heads = [h.reshape(1, 1) for h in (head_bias, head_moment, head_second)]
    smalls = [norm_params, norm_moment, norm_second, end_params, end_moment, end_second] + heads
    out = last_update(
        me,
        jnp.stack([correction, count]),
        everyone,
        smalls,
        bases,
        late,
        (kernels[0], kernel_moment[0], kernel_second[0]),
        kernel_rate,
    )
    return (
        (out[3].reshape(()), out[4].reshape(()))
        + tuple(k[None] for k in out[:3])
        + tuple(out[5:11])
        + tuple(h.reshape(1) for h in out[11:14])
        + (final[0], final[1])
    )


def solution(mesh):
    rows = P("dp", None, "tile", None)
    kern = P(None, "dp", None)
    state = P(None, "dp", "tile", None, None)
    placed = (rows, rows, rows, P("dp"), P(), kern, kern, kern) + (P(),) * 9 + (state, state)
    outs = (P(), P(), kern, kern, kern) + (P(),) * 9 + (state, state)
    return jax.shard_map(
        per_device, mesh=mesh, in_specs=placed, out_specs=outs, check_vma=False
    )
```

```python
import math

import jax
import jax.numpy as jnp
from jax import lax
from jax.experimental import pallas as pl
from jax.experimental.pallas import tpu as pltpu
from jax.sharding import PartitionSpec as P

IN_DIM = 512
KERNEL = 5
GROUP_SIZE = 64
MARGIN = KERNEL // 2
TAPS = KERNEL * KERNEL
ONES_ROW = 32

clip_limit = 0.005
small_rate = 0.1
BF = jnp.bfloat16
F32 = jnp.float32
I32 = jnp.int32
EXACT = lax.Precision.HIGHEST


def spread(x, axes):
    n = lax.axis_size(axes)
    return lax.all_to_all(jnp.broadcast_to(x[None], (n,) + x.shape), axes, 0, 0)


def shape(dims, kind):
    return jax.ShapeDtypeStruct(dims, kind)


def hint(microseconds):
    return pl.CostEstimate(
        flops=int(microseconds * 0.35 * 1e9), bytes_accessed=int(microseconds * 0.35 * 3e6), transcendentals=0
    )


def whole(array):
    dims = array.shape
    return pl.BlockSpec(dims, lambda *unused: (0,) * len(dims))


def after(value, *others):
    def body(*refs):
        pass

    anywhere = pl.BlockSpec(memory_space=pl.ANY)
    return pl.pallas_call(
        body,
        out_shape=shape(value.shape, value.dtype),
        in_specs=[anywhere] * (1 + len(others)),
        out_specs=anywhere,
        input_output_aliases={0: 0},
        name="after",
    )(value, *others)


def columns_kernel(place, first, second, third, fourth, out):
    odd = place[1] == 1
    lower = lax.broadcasted_iota(I32, first.shape, 1) < GROUP_SIZE

    def pair(left, right):
        x, y = left[...], right[...]
        low = jnp.where(odd, pltpu.roll(x, GROUP_SIZE, 1), x)
        high = jnp.where(odd, y, pltpu.roll(y, GROUP_SIZE, 1))
        return jnp.where(lower, low, high).astype(BF)

    out[:, : 2 * GROUP_SIZE] = pair(first, second)
    out[:, 2 * GROUP_SIZE :] = pair(third, fourth)


def own_kernel_columns(kernels, block):
    own, gate_dim = kernels.shape
    lanes = 2 * GROUP_SIZE
    per_quarter = gate_dim // 4 // lanes
    steps = 2 if own % 32 == 0 else 5
    step = own // steps
    place = jnp.stack([block // 2, block % 2]).astype(I32)

    def spec(quarter):
        return pl.BlockSpec((step, lanes), lambda i, where: (i, quarter * per_quarter + where[0]))

    return pl.pallas_call(
        columns_kernel,
        out_shape=shape((own, 4 * GROUP_SIZE), BF),
        grid_spec=pltpu.PrefetchScalarGridSpec(
            num_scalar_prefetch=1,
            grid=(steps,),
            in_specs=[spec(q) for q in range(4)],
            out_specs=pl.BlockSpec((step, 4 * GROUP_SIZE), lambda i, where: (i, 0)),
        ),
        name="columns",
    )(place, kernels, kernels, kernels, kernels)


def group_mean(values):
    n = values.shape[1]
    same = (
        lax.broadcasted_iota(I32, (n, n), 0) // GROUP_SIZE
        == lax.broadcasted_iota(I32, (n, n), 1) // GROUP_SIZE
    )
    mixer = jnp.where(same, 1.0 / GROUP_SIZE, 0.0).astype(F32)
    return jnp.dot(values, mixer, precision=EXACT, preferred_element_type=F32)


def fill_bands(bands, image, columns, mirrored=False):
    pixels, depth = image.shape
    edge = MARGIN * columns
    column = lax.broadcasted_iota(I32, image.shape, 0) % columns
    blank = jnp.zeros((edge, depth), BF)
    for d in range(KERNEL):
        move = (MARGIN - d) if mirrored else (d - MARGIN)
        lanes = slice(d * depth, (d + 1) * depth)
        moved = image if move == 0 else pltpu.roll(image, (-move) % pixels, 0)
        inside = (column + move >= 0) & (column + move < columns)
        bands[edge : edge + pixels, lanes] = jnp.where(inside, moved, 0.0).astype(BF)
        bands[:edge, lanes] = blank
        bands[edge + pixels :, lanes] = blank


def cell_parts(gates, cells_prev, gain, shift):
    width = cells_prev.shape[1]
    centred = gates - group_mean(gates)
    inverse = lax.rsqrt(group_mean(centred * centred) + 1e-05)
    norm = centred * inverse
    normed = norm * gain + shift
    input_gate = jax.nn.sigmoid(normed[:, :width])
    forget_gate = jax.nn.sigmoid(normed[:, width : 2 * width])
    candidate = jnp.tanh(normed[:, 2 * width : 3 * width])
    output_gate = jax.nn.sigmoid(normed[:, 3 * width :])
    cells = forget_gate * cells_prev + input_gate * candidate
    return norm, inverse, input_gate, forget_gate, candidate, output_gate, cells


def fetch_shards(parts, where, near, arrived):
    if len(parts) == 1:
        for k in range(KERNEL):
            shard_row(parts[0], near, arrived, k).start()
        return
    rows = parts[0].shape[0]
    for k, part in enumerate(parts):
        @pl.when(where[k] >= 0)
        def start():
            begin = pl.multiple_of(where[k] * rows, 16)
            pltpu.make_async_copy(
                part, near.at[pl.ds(begin, rows), :], arrived.at[where[k]]
            ).start()


def shard_row(part, near, arrived, step):
    depth = KERNEL * IN_DIM
    rows = pl.ds(pl.multiple_of(step * depth, depth), depth)
    return pltpu.make_async_copy(part.at[rows, :], near.at[rows, :], arrived.at[step])


def await_shards(parts, near, arrived):
    if len(parts) > 1:
        rows = parts[0].shape[0]
        for k in range(near.shape[0] // rows):
            pltpu.make_async_copy(
                parts[0], near.at[pl.ds(k * rows, rows), :], arrived.at[k]
            ).wait()


def await_row(parts, near, arrived, step):
    if len(parts) == 1:
        shard_row(parts[0], near, arrived, step).wait()


def shard_scratch(parts):
    rows, gate = parts[0].shape
    count = KERNEL if len(parts) == 1 else TAPS * IN_DIM // rows
    return [pltpu.VMEM((TAPS * IN_DIM, gate), BF), pltpu.SemaphoreType.DMA((count,))]


def half_taps(near, step, first, depth):
    taps = []
    for d in range(KERNEL):
        row = (step * KERNEL + d) * IN_DIM + first
        taps.append(near[pl.ds(pl.multiple_of(row, 16), depth), :])
    return jnp.concatenate(taps, axis=1)


def forward_kernel(columns, count, first_row, where, obs, hid, ends, cells_prev, norms, head, *refs):
    many = count > 1
    shards, refs = refs[:count], refs[-12:] if many else refs[-10:]
    gates_out, cells_out, hidden_out, low_out, turned_out, seen_out = refs[:6]
    bands, total, near, arrived = refs[7:11] if many else refs[6:]
    pixels = total.shape[0]
    fetch_shards(shards, where, near, arrived)
    lifted = (ends[0:1, :] * obs[...] + ends[1:2, :]).astype(BF).astype(F32)
    fill_bands(bands, jnp.concatenate([lifted, hid[...].astype(F32)], axis=1), columns)
    total[...] = jnp.zeros_like(total)
    await_shards(shards, near, arrived)
    if many:
        ordered = pltpu.make_async_copy(near, refs[6], refs[11])
        ordered.start()

    @pl.loop(0, KERNEL)
    def tap_row(step):
        begin = pl.multiple_of((first_row[0] + step) * columns, columns)
        depth = KERNEL * IN_DIM
        await_row(shards, near, arrived, step)
        rows = pl.ds(pl.multiple_of(step * depth, depth), depth)
        total[...] += jnp.dot(
            bands[pl.ds(begin, pixels), :], near[rows, :], preferred_element_type=F32
        )

    gates = total[...]
    parts = cell_parts(gates, cells_prev[...], norms[0:1, :], norms[1:2, :])
    output_gate, cells = parts[5], parts[6]
    hidden = output_gate * jnp.tanh(cells)
    gates_out[...] = gates
    cells_out[...] = cells
    hidden_out[...] = hidden
    low_out[...] = hidden.astype(BF)
    turned_out[...] = jnp.broadcast_to(jnp.transpose(hidden).astype(BF)[None], turned_out.shape)
    seen_out[...] = lax.dot_general(
        head[...], hidden, (((1,), (1,)), ((), ())), precision=EXACT, preferred_element_type=F32
    )[0:1, :]
    if many:
        ordered.wait()


def forward_frame(
    copies, columns, first_row, where, obs, hid, ends, parts, cells_prev, norms, head, waits
):
    pixels, width = cells_prev.shape
    image = hid.shape[0]
    gate = 4 * width
    outs = (
        shape((pixels, gate), F32),
        shape((pixels, width), F32),
        shape((pixels, width), F32),
        shape((pixels, width), BF),
        shape((copies, width, pixels), BF),
        shape((1, pixels), F32),
    )
    args = [obs, hid, ends, cells_prev, norms, head]
    far = list(parts) + list(waits)
    out_specs = [whole(o) for o in outs]
    scratch = [
        pltpu.VMEM((image + 2 * MARGIN * columns, KERNEL * IN_DIM), BF),
        pltpu.VMEM((pixels, gate), F32),
    ] + shard_scratch(parts)
    if len(parts) > 1:
        outs += (shape((TAPS * IN_DIM, gate), BF),)
        out_specs.append(pl.BlockSpec(memory_space=pl.ANY))
        scratch.append(pltpu.SemaphoreType.DMA)

    def body(*refs):
        forward_kernel(columns, len(parts), *refs)

    return pl.pallas_call(
        body,
        out_shape=outs,
        grid_spec=pltpu.PrefetchScalarGridSpec(
            num_scalar_prefetch=2,
            grid=(1,),
            in_specs=[whole(a) for a in args] + [pl.BlockSpec(memory_space=pl.ANY)] * len(far),
            out_specs=out_specs,
            scratch_shapes=scratch,
        ),
        cost_estimate=hint(4),
        name="forward_frame",
    )(first_row, where, *args, *far)


def backward_kernel(last, *refs):
    (scalars, seen, target, valid, gates, cells_prev, norms, head, looks) = refs[:9]
    grad_next, pieces = (None, ()) if last else (refs[9], refs[10:-6])
    low_out, cells_grad, sums_out, echo_out, rows_out, head_out = refs[-6:]
    pixels, width = cells_prev.shape
    gain = norms[0:1, :]
    error = jnp.sum(seen[...], axis=0, keepdims=True) + scalars[0] - target[...]
    weighted = valid[...] * error
    grad_row = 2.0 * weighted / scalars[1]
    rows_out[0:1, :] = grad_row
    rows_out[1:2, :] = weighted * error
    rows_out[2:8, :] = jnp.zeros((6, pixels), F32)
    grad_pred = jnp.transpose(jnp.broadcast_to(grad_row, (2 * GROUP_SIZE, pixels)))[:, :width]

    norm, inverse, input_gate, forget_gate, candidate, output_gate, cells = cell_parts(
        gates[...], cells_prev[...], gain, norms[1:2, :]
    )
    squashed = jnp.tanh(cells)
    grad_hidden = grad_pred * head[0:1, :]
    for piece in pieces:
        grad_hidden = grad_hidden + piece[...]
    head_out[...] = jnp.broadcast_to(
        jnp.sum(grad_pred * (output_gate * squashed), axis=0, keepdims=True), head_out.shape
    )
    grad_cells = grad_hidden * output_gate * (1.0 - squashed * squashed)
    if not last:
        grad_cells = grad_cells + grad_next[...]
    cells_grad[...] = grad_cells * forget_gate
    grad_normed = jnp.concatenate(
        [
            grad_cells * candidate * input_gate * (1.0 - input_gate),
            grad_cells * cells_prev[...] * forget_gate * (1.0 - forget_gate),
            grad_cells * input_gate * (1.0 - candidate * candidate),
            grad_hidden * squashed * output_gate * (1.0 - output_gate),
        ],
        axis=1,
    )
    sums_out[0:1, :] = jnp.sum(grad_normed * norm, axis=0, keepdims=True)
    sums_out[1:2, :] = jnp.sum(grad_normed, axis=0, keepdims=True)
    sums_out[2:8, :] = jnp.zeros((6, 4 * width), F32)
    scaled = grad_normed * gain
    grad_gates = inverse * (scaled - group_mean(scaled) - norm * group_mean(scaled * norm))
    low = grad_gates.astype(BF)
    low_out[...] = jnp.broadcast_to(low[None], low_out.shape)
    echo_out[...] = jnp.dot(
        looks[...], low.astype(F32), precision=EXACT, preferred_element_type=F32
    )


def backward_frame(
    copies, scalars, seen, target, valid, gates, cells_prev, norms, head, looks, later
):
    pixels, width = cells_prev.shape
    gate = 4 * width
    outs = (
        shape((copies, pixels, gate), BF),
        shape((pixels, width), F32),
        shape((8, gate), F32),
        shape((looks.shape[0], gate), F32),
        shape((8, pixels), F32),
        shape((8, width), F32),
    )
    args = [seen, target, valid, gates, cells_prev, norms, head, looks] + list(later)
    last = not later

    def body(*refs):
        backward_kernel(last, *refs)

    return pl.pallas_call(
        body,
        out_shape=outs,
        in_specs=[pl.BlockSpec(memory_space=pltpu.SMEM)] + [whole(a) for a in args],
        out_specs=[whole(o) for o in outs],
        grid=(1,),
        cost_estimate=hint(4),
        name="backward_cell",
    )(scalars, *args)


def hidden_kernel(columns, count, me, where, above, low, below, *refs):
    shards, outs = refs[:count], refs[count:-5]
    bands, total, held, near, arrived = refs[-5:]
    pixels = low.shape[1]
    blocks, unused, width = held.shape
    fetch_shards(shards, where, near, arrived)
    fill_bands(bands, low[0].astype(F32), columns, mirrored=True)
    edge = MARGIN * columns
    if above is not None:
        for side, place in ((above, 0), (below, edge + pixels)):
            image = side[...].astype(F32)
            column = lax.broadcasted_iota(I32, image.shape, 0) % columns
            depth = image.shape[1]
            for d in range(KERNEL):
                move = MARGIN - d
                moved = image if move == 0 else pltpu.roll(image, (-move) % edge, 0)
                inside = (column + move >= 0) & (column + move < columns)
                bands[place : place + edge, d * depth : (d + 1) * depth] = jnp.where(
                    inside, moved, 0.0
                ).astype(BF)
    total[...] = jnp.zeros_like(total)
    hidden_dim = total.shape[1]
    await_shards(shards, near, arrived)

    @pl.loop(0, KERNEL)
    def tap_row(step):
        begin = pl.multiple_of((KERNEL - 1 - step) * columns, columns)
        await_row(shards, near, arrived, step)
        taps = half_taps(near, step, IN_DIM - hidden_dim, hidden_dim)
        total[...] += lax.dot_general(
            bands[pl.ds(begin, pixels), :],
            taps,
            (((1,), (1,)), ((), ())),
            preferred_element_type=F32,
        )

    for b in range(blocks):
        held[jnp.bitwise_xor(b, me[0])] = total[:, b * width : (b + 1) * width]
    for k in range(blocks):
        outs[k][...] = held[k]


def hidden_gradient(columns, blocks, me, where, sides, low, parts):
    unused, pixels, gate = low.shape
    hidden_dim = IN_DIM // 2
    width = hidden_dim // blocks
    outs = (shape((pixels, width), F32),) * blocks
    args = [low] if sides is None else [sides[0], low, sides[1]]
    specs = [
        pl.BlockSpec((1,) + a.shape[1:], lambda *i: (0, 0, 0)) if a is low else whole(a)
        for a in args
    ]

    def body(me_ref, where_ref, *refs):
        if sides is None:
            refs = (None, refs[0], None) + refs[1:]
        hidden_kernel(columns, len(parts), me_ref, where_ref, *refs)

    return pl.pallas_call(
        body,
        out_shape=outs,
        grid_spec=pltpu.PrefetchScalarGridSpec(
            num_scalar_prefetch=2,
            grid=(1,),
            in_specs=specs + [pl.BlockSpec(memory_space=pl.ANY)] * len(parts),
            out_specs=[whole(o) for o in outs],
            scratch_shapes=[
                pltpu.VMEM((pixels + 2 * MARGIN * columns, KERNEL * gate), BF),
                pltpu.VMEM((pixels, hidden_dim), F32),
                pltpu.VMEM((blocks, pixels, width), F32),
            ]
            + shard_scratch(parts),
        ),
        cost_estimate=hint(4),
        name="hidden_gradient",
    )(me, where, *args, *parts)


def lift_kernel(where, echo, *refs):
    shards, (out, near, arrived) = refs[:-3], refs[-3:]
    fetch_shards(shards, where, near, arrived)
    out[...] = jnp.zeros_like(out)
    await_shards(shards, near, arrived)
    hidden_dim = out.shape[1]

    @pl.loop(0, KERNEL)
    def tap_row(step):
        await_row(shards, near, arrived, step)
        lanes = []
        for d in range(KERNEL):
            rows = []
            for place in (step * KERNEL + d, step * KERNEL + d + ONES_ROW):
                value = echo[pl.ds(place, 1), :]
                high = value.astype(BF).astype(F32)
                rows += [high, value - high]
            rows.append(jnp.zeros((12, echo.shape[1]), F32))
            lanes.append(jnp.concatenate(rows, axis=0).astype(BF))
        out[...] += lax.dot_general(
            jnp.concatenate(lanes, axis=1),
            half_taps(near, step, 0, hidden_dim),
            (((1,), (1,)), ((), ())),
            preferred_element_type=F32,
        )


def lift_gradients(where, echo, parts, waits):
    hidden_dim = IN_DIM // 2
    count = len(parts)

    def body(where_ref, echo_ref, *refs):
        lift_kernel(where_ref, echo_ref, *refs[:count], *refs[-3:])

    far = list(parts) + list(waits)
    got = pl.pallas_call(
        body,
        out_shape=shape((16, hidden_dim), F32),
        grid_spec=pltpu.PrefetchScalarGridSpec(
            num_scalar_prefetch=1,
            grid=(1,),
            in_specs=[whole(echo)] + [pl.BlockSpec(memory_space=pl.ANY)] * len(far),
            out_specs=pl.BlockSpec((16, hidden_dim), lambda *i: (0, 0)),
            scratch_shapes=shard_scratch(parts),
        ),
        cost_estimate=hint(5),
        name="lift_gradients",
    )(where, echo, *far)
    return jnp.stack([got[0] + got[1], got[2] + got[3]])


def patches_kernel(columns, slabs, tiles, places, obs, ends, *refs):
    hid, (out, moves, patches, held) = refs[:tiles], refs[tiles:]
    own, image = out.shape
    span = moves.shape[0]
    for k in range(tiles):
        held[k] = hid[k][0]

    @pl.when(pl.program_id(0) == 0)
    def start():
        source = lax.broadcasted_iota(I32, (image, image), 0)
        target = lax.broadcasted_iota(I32, (image, image), 1)
        for k in range(span):
            row_off, col_off = places[2 + 2 * k], places[3 + 2 * k]
            column = target % columns + col_off
            hit = source == target + row_off * columns + col_off
            hit = hit & (column >= 0) & (column < columns)
            moves[k] = jnp.where(hit, 1.0, 0.0).astype(BF)

    lifted = (ends[:, 0:1] * obs[0] + ends[:, 1:2]).astype(BF)
    blocks = tiles // slabs
    parts = [lifted]
    for b in range(blocks):
        piece = [held[jnp.bitwise_xor(s * blocks + b, places[1])] for s in range(slabs)]
        parts.append(piece[0] if slabs == 1 else jnp.concatenate(piece, axis=1))
    joined = jnp.concatenate(parts, axis=0)
    for k in range(span):
        patches[k * IN_DIM : (k + 1) * IN_DIM, :] = jnp.dot(
            joined, moves[k], preferred_element_type=F32
        ).astype(BF)
    skip = pl.multiple_of(places[0], 16)
    out[...] = patches[pl.ds(skip, own), :]


def owned_patches(columns, slabs, own, span, places, obs, hid, ends, waits):
    owners, unused, image = obs.shape
    tiles, (unused_too, width, pixels) = len(hid), hid[0].shape

    n = 3 + tiles

    def body(*refs):
        patches_kernel(columns, slabs, tiles, *refs[:n], *refs[n + len(waits) :])

    return pl.pallas_call(
        body,
        out_shape=shape((own, owners * image), BF),
        grid_spec=pltpu.PrefetchScalarGridSpec(
            num_scalar_prefetch=1,
            grid=(owners,),
            in_specs=[
                pl.BlockSpec((1, 1, image), lambda s, where: (s, 0, 0)),
                whole(ends),
            ]
            + [pl.BlockSpec((1, width, pixels), lambda s, where: (s, 0, 0))] * tiles
            + [pl.BlockSpec(memory_space=pl.ANY)] * len(waits),
            out_specs=pl.BlockSpec((own, image), lambda s, where: (0, s)),
            scratch_shapes=[
                pltpu.VMEM((span, image, image), BF),
                pltpu.VMEM((span * IN_DIM, image), BF),
                pltpu.VMEM((tiles, width, pixels), BF),
            ],
        ),
        cost_estimate=hint(9),
        name="owned_patches",
    )(places, obs, ends, *hid, *waits)


def adamw(weight, moment, second, grad, rate, correction):
    moment_new = 0.5 * moment + 0.5 * grad
    second_new = 0.5 * second + 0.5 * grad * grad
    update = moment_new / correction / (jnp.sqrt(second_new / correction) + 1e-08)
    return (weight - rate * (update + 0.01 * weight), moment_new, second_new)


def rows_at_once(own):
    return 16 * math.gcd(own // 16, 20)


def patch_dot(patch, pieces):
    flat = [p[...].reshape(patch.shape[1], p.shape[2]) for p in pieces]
    signal = flat[0] if len(flat) == 1 else jnp.concatenate(flat, axis=1)
    return jnp.dot(patch[...], signal, preferred_element_type=F32)


def gradient_kernel(blocks, squared, patch, *refs):
    pieces, refs = refs[:blocks], refs[blocks:]
    grad = patch_dot(patch, pieces)
    gate = pieces[0].shape[2]
    if squared:
        base, grad_out, square_out = refs
        grad = grad + base[...]

        @pl.when(pl.program_id(0) == 0)
        def start():
            square_out[...] = jnp.zeros_like(square_out)

        lanes = square_out.shape[1]
        square = grad * grad
        square = square[:, :lanes] + square[:, lanes:]
        square_out[...] += jnp.sum(square, axis=0, keepdims=True)
        grad_out[...] = grad
    else:
        for k in range(blocks):
            refs[k][...] = grad[:, k * gate : (k + 1) * gate]


def patch_gradient(patch, pieces, base=None, waits=()):
    own, gate = patch.shape[0], pieces[0].shape[2]
    step = own // 2
    rows = pl.BlockSpec((step, gate), lambda i: (i, 0))
    outs = [shape((own, gate), F32) for p in pieces]
    out_specs = [rows] * len(pieces)
    args = [patch] + list(pieces)
    in_specs = [pl.BlockSpec((step, patch.shape[1]), lambda i: (i, 0))] + [whole(p) for p in pieces]
    if base is not None:
        args, in_specs = args + [base], in_specs + [rows]
        outs = outs + [shape((1, gate // 2), F32)]
        out_specs = out_specs + [pl.BlockSpec((1, gate // 2), lambda i: (0, 0))]

    n = len(args)
    args, in_specs = args + list(waits), in_specs + [pl.BlockSpec(memory_space=pl.ANY)] * len(waits)

    def body(*refs):
        gradient_kernel(len(pieces), base is not None, *refs[:n], *refs[n + len(waits) :])

    return pl.pallas_call(
        body,
        out_shape=tuple(outs),
        grid=(own // step,),
        in_specs=in_specs,
        out_specs=out_specs,
        compiler_params=pltpu.CompilerParams(vmem_limit_bytes=60 << 20),
        cost_estimate=hint(3 + 2 * len(pieces)),
        name="patch_gradient",
    )(*args)


def small_update(scalars, everyone, triples, factor_row, smalls_out, measures_out):
    total = jnp.sum(everyone[...], axis=0)
    lanes = total.shape[1]
    gate_dim, hidden_dim = triples[0].shape[2], triples[3].shape[1]
    norm_rows = 2 * gate_dim // lanes
    end_rows = 3 * hidden_dim // lanes
    last = norm_rows + end_rows
    row = lax.broadcasted_iota(I32, total.shape, 0)
    lane = lax.broadcasted_iota(I32, total.shape, 1)
    wide = (row < last) | ((row == last) & (lane == 0))
    alone = row == last + 1
    squares = jnp.where(wide, total * total, jnp.where(alone, total, 0.0))
    grad_norm = jnp.sqrt(jnp.sum(jnp.sum(squares, axis=0, keepdims=True), axis=1, keepdims=True))
    factor = clip_limit / jnp.maximum(grad_norm, clip_limit)
    factor_row[...] = jnp.broadcast_to(factor, factor_row.shape)
    measures_out[0][...] = total[last : last + 1, 1:2] / scalars[1]
    measures_out[1][...] = grad_norm

    def line(begin, length):
        return jnp.concatenate([total[r : r + 1, :] for r in range(begin, begin + length)], axis=1)

    def update(place, grad, index):
        found = [t[index] for t in triples[place : place + 3]]
        got = adamw(*found, grad * factor, small_rate, scalars[0])
        for out, value in zip(smalls_out[place : place + 3], got):
            out[index] = value

    for r in range(2):
        update(0, line(r * norm_rows // 2, norm_rows // 2), r)
    for r in range(3):
        update(3, line(norm_rows + r * end_rows // 3, end_rows // 3), slice(r, r + 1))
    update(6, total[last : last + 1, 0:1], slice(0, 1))


def last_kernel(blocks, extra, rate, me, scalars, everyone, *refs):
    triples, refs = refs[:9], refs[9:]
    bases, refs = refs[:blocks], refs[blocks:]
    pieces, refs = refs[:extra], refs[extra:]
    held, factor_row = refs[-2:]
    weight, moment, second, weight_out, moment_out, second_out = refs[:6]
    measures_out, smalls_out = refs[6:8], refs[8:17]

    @pl.when(pl.program_id(0) == 0)
    def start():
        small_update(scalars, everyone, triples, factor_row, smalls_out, measures_out)

    for k in range(blocks):
        held[k] = bases[k][...]
    if extra:
        patch, pieces = pieces[0], pieces[1:]
        grad = patch_dot(patch, pieces)
        gate = held.shape[2]
        for k in range(1, blocks):
            held[k] += grad[:, (k - 1) * gate : k * gate]
    width = held.shape[2] // 4
    placed = [held[jnp.bitwise_xor(b, me[0])] for b in range(blocks)]
    for q in range(4):
        grad = jnp.concatenate([p[:, q * width : (q + 1) * width] for p in placed], axis=1)
        cols = slice(q * blocks * width, (q + 1) * blocks * width)
        weight_out[:, cols], moment_out[:, cols], second_out[:, cols] = adamw(
            weight[:, cols], moment[:, cols], second[:, cols], grad * factor_row[...], rate,
            scalars[0],
        )


def last_update(me, scalars, everyone, smalls, bases, late, kernel_triple, rate):
    own, gate_dim = kernel_triple[0].shape
    blocks = len(bases)
    step = rows_at_once(own)
    gate = gate_dim // blocks
    wide = pl.BlockSpec((step, gate_dim), lambda i, where: (i, 0))
    thin = pl.BlockSpec((step, gate), lambda i, where: (i, 0))
    late_specs = []
    if late:
        late_specs = [pl.BlockSpec((step, late[0].shape[1]), lambda i, where: (i, 0))]
        late_specs += [whole(p) for p in late[1:]]
    measures = [shape((1, 1), F32)] * 2

    def body(*refs):
        n = 3 + 9 + blocks + len(late)
        ins, outs = refs[: n + 3], refs[n + 3 :]
        last_kernel(blocks, len(late), rate, *ins, *outs)

    return pl.pallas_call(
        body,
        out_shape=tuple([shape((own, gate_dim), F32)] * 3 + measures + [shape(t.shape, F32) for t in smalls]),
        grid_spec=pltpu.PrefetchScalarGridSpec(
            num_scalar_prefetch=1,
            grid=(own // step,),
            in_specs=[pl.BlockSpec(memory_space=pltpu.SMEM), whole(everyone)]
            + [whole(t) for t in smalls]
            + [thin] * blocks
            + late_specs
            + [wide] * 3,
            out_specs=[wide] * 3 + [whole(m) for m in measures] + [whole(t) for t in smalls],
            scratch_shapes=[
                pltpu.VMEM((blocks, step, gate), F32),
                pltpu.VMEM((1, gate_dim // 4), F32),
            ],
        ),
        compiler_params=pltpu.CompilerParams(vmem_limit_bytes=60 << 20),
        cost_estimate=hint(22),
        name="last_update",
    )(me, scalars, everyone, *smalls, *bases, *late, *kernel_triple)


def split_states(me, blocks, hidden, cells, waits):
    pixels, width = hidden.shape
    rows = pixels // blocks

    def body(me_ref, hidden_ref, cells_ref, *refs):
        for k, out in enumerate(refs[len(waits) :]):
            begin = pl.multiple_of(jnp.bitwise_xor(me_ref[0], k) * rows, rows)
            out[0] = hidden_ref[pl.ds(begin, rows), :]
            out[1] = cells_ref[pl.ds(begin, rows), :]

    outs = (shape((2, rows, width), F32),) * blocks
    return list(
        pl.pallas_call(
            body,
            out_shape=outs,
            grid_spec=pltpu.PrefetchScalarGridSpec(
                num_scalar_prefetch=1,
                grid=(1,),
                in_specs=[whole(hidden), whole(cells)]
                + [pl.BlockSpec(memory_space=pl.ANY)] * len(waits),
                out_specs=[whole(o) for o in outs],
            ),
            name="split_states",
        )(me, hidden, cells, *waits)
    )


def join_states(me, parts, waits):
    blocks = len(parts)
    unused, rows, width = parts[0].shape

    def body(me_ref, *refs):
        outs, held = refs[-3:-1], refs[-1]
        for k in range(blocks):
            held[jnp.bitwise_xor(me_ref[0], k)] = refs[k][...]
        for n, out in enumerate(outs):
            out[...] = jnp.concatenate([held[b, n] for b in range(blocks)], axis=1)

    outs = (shape((rows, blocks * width), F32),) * 2
    return pl.pallas_call(
        body,
        out_shape=outs,
        grid_spec=pltpu.PrefetchScalarGridSpec(
            num_scalar_prefetch=1,
            grid=(1,),
            in_specs=[whole(p) for p in parts]
            + [pl.BlockSpec(memory_space=pl.ANY)] * len(waits),
            out_specs=[whole(o) for o in outs],
            scratch_shapes=[pltpu.VMEM((blocks, 2, rows, width), F32)],
        ),
        name="join_states",
    )(me, *parts, *waits)


def looks_kernel(height, columns, obs, out):
    lane = lax.broadcasted_iota(I32, (1, height * columns), 1)
    for f in range(out.shape[0]):
        out[f] = jnp.zeros(out.shape[1:], F32)
        values = obs[f]
        for t in range(TAPS):
            down, right = t // KERNEL - MARGIN, t % KERNEL - MARGIN
            row, column = lane // columns + down, lane % columns + right
            inside = (row >= 0) & (row < height) & (column >= 0) & (column < columns)
            offset = down * columns + right
            moved = values if offset == 0 else pltpu.roll(values, (-offset) % values.shape[1], 1)
            out[f, t : t + 1, :] = jnp.where(inside, moved, 0.0)
            out[f, ONES_ROW + t : ONES_ROW + t + 1, :] = jnp.where(inside, 1.0, 0.0)


def tap_looks(height, columns, obs):
    out = shape((obs.shape[0], 2 * ONES_ROW, height * columns), F32)

    def body(*refs):
        looks_kernel(height, columns, *refs)

    return pl.pallas_call(
        body, out_shape=out, grid=(1,), in_specs=[whole(obs)], out_specs=whole(out), name="looks"
    )(obs)


def per_device(
    observed,
    targets,
    pixel_mask,
    lengths,
    step_count,
    kernels,
    kernel_moment,
    kernel_second,
    norm_params,
    norm_moment,
    norm_second,
    end_params,
    end_moment,
    end_second,
    head_bias,
    head_moment,
    head_second,
    hidden_init,
    cells_init,
):
    tiles, owners = lax.axis_size("tile"), lax.axis_size("dp")
    streams, frames, tile_rows, columns = observed.shape
    height = tile_rows * tiles
    hidden_dim = end_params.shape[1]
    gate_dim = 4 * hidden_dim
    blocks = math.gcd(tiles, hidden_dim // GROUP_SIZE)
    slabs = tiles // blocks
    rows = height // slabs
    width = hidden_dim // blocks
    gate = 4 * width
    pixels, image = rows * columns, height * columns
    own = kernels.shape[1]
    assert streams == 1 and width == GROUP_SIZE and own % 80 == 0 and pixels == gate
    tile = lax.axis_index("tile")
    owner = lax.axis_index("dp")
    block, slab = tile % blocks, tile // blocks
    first_row = slab * rows
    groups = None
    if slabs > 1:
        groups = [[s * blocks + b for b in range(blocks)] for s in range(slabs)]

    local = own_kernel_columns(kernels[0], block)

    frame_ids = lax.broadcasted_iota(I32, (1, frames), 1)
    counted = (frame_ids < lengths[:, None]).astype(F32)
    valid = pixel_mask.astype(F32) * counted[:, :, None, None]
    small = spread(jnp.stack([observed[0], targets[0], valid[0]]), ("dp", "tile"))
    small = small.reshape(owners, tiles, 3, frames, tile_rows * columns)
    small = small.transpose(2, 3, 0, 1, 4).reshape(3, frames, owners, image)
    count = jnp.maximum(jnp.sum(small[2]), 1.0)
    obs_all = small[0]
    mine = lax.dynamic_slice_in_dim(small, owner, 1, 2)
    mine_rows = lax.dynamic_slice_in_dim(mine, first_row * columns, pixels, 3)

    looks = tap_looks(height, columns, mine[0])
    if slabs > 1:
        looks = lax.dynamic_slice_in_dim(looks, first_row * columns, pixels, 2)

    def own_columns(values):
        shaped = values.reshape(values.shape[:-1] + (4, hidden_dim))
        part = lax.dynamic_slice_in_dim(shaped, block * width, width, values.ndim)
        return part.reshape(values.shape[:-1] + (gate,))

    norms = own_columns(norm_params[:, 0])
    head = lax.dynamic_slice_in_dim(end_params[2], block * width, width, 0)
    head = jnp.broadcast_to(head[None], (8, width))
    ends = end_params[:2]
    ends_turned = ends.T

    me = jnp.reshape(block if slabs == 1 else jnp.zeros_like(block), (1,)).astype(I32)

    def all_tiles(values, between=()):
        if slabs > 1:
            got = lax.all_gather(values, "tile")
            return [got[k] for k in range(tiles)]
        held, order, stride = [values], [0], tiles // 2
        while stride:
            pairs = [(j, j ^ stride) for j in range(tiles)]
            held = held + [lax.ppermute(h, "tile", pairs) for h in held]
            if between and stride > 1:
                held[1:] = [after(h, *between) for h in held[1:]]
            order = order + [k ^ stride for k in order]
            stride //= 2
        return [held[order.index(k)] for k in range(tiles)]

    span = max((own * (i + 1) - 1) // IN_DIM - own * i // IN_DIM + 1 for i in range(owners))
    first_tap = jnp.minimum(owner * own // IN_DIM, TAPS - span)
    places = [owner * own - first_tap * IN_DIM, me[0]]
    for k in range(span):
        places += [(first_tap + k) // KERNEL - MARGIN, (first_tap + k) % KERNEL - MARGIN]
    places = jnp.stack(places).astype(I32)

    def patches_of(frame_no, hid, waits=()):
        obs_rows = obs_all[frame_no].reshape(owners, 1, image)
        return owned_patches(
            columns, slabs, own, span, places, obs_rows, hid, ends_turned, waits
        )

    states = jnp.stack([hidden_init[0, 0], cells_init[0, 0]])
    states = states.reshape(2, tile_rows * columns, blocks, width).transpose(2, 0, 1, 3)
    states = lax.all_to_all(states, "tile", 0, 0, axis_index_groups=groups)
    states = states.transpose(1, 0, 2, 3).reshape(2, pixels, width)
    low = states[0].astype(BF)
    cells = states[1]
    patches = [None] * frames

    def whole_hidden(values):
        got = lax.all_gather(values, "tile").reshape(slabs, blocks, pixels, width)
        return got.transpose(0, 2, 1, 3).reshape(image, hidden_dim)

    heads = [h.reshape(1, 1) for h in (head_bias, head_moment, head_second)]
    hid = whole_hidden(low)
    parts = [lax.all_gather(local, "dp", axis=0, tiled=True)]
    where = jnp.zeros((1,), I32)
    patches[0] = patches_of(0, all_tiles(spread(low.T, "dp")))
    first = jnp.reshape(first_row, (1,)).astype(I32)
    kept, seen, turns = [], [], [None] * frames
    for frame_no in range(frames):
        obs_column = mine[0, frame_no].reshape(image, 1)
        gates, cells_next, hidden, low_next, turned, seen_part, *ordered = forward_frame(
            owners,
            columns,
            first,
            where,
            obs_column,
            hid,
            ends,
            parts,
            cells,
            norms,
            head,
            [patches[0], looks] + heads if frame_no == 0 else [],
        )
        if ordered:
            parts, where = ordered, jnp.zeros((1,), I32)
        kept.append((gates, cells))
        cells = cells_next
        seen.append(seen_part[0])
        if frame_no + 1 < frames:
            turns[frame_no + 1] = lax.all_to_all(turned, "dp", 0, 0)
            hid = whole_hidden(low_next)
    seen = lax.all_gather(jnp.stack(seen), "tile", axis_index_groups=groups)
    seen, turns[1:] = lax.optimization_barrier((seen, turns[1:]))
    turns[1:] = [all_tiles(t) for t in turns[1:]]
    scalars = jnp.stack([head_bias[0], count])

    sums = jnp.zeros((8, gate), F32)
    echo = jnp.zeros((2 * ONES_ROW, gate), F32)
    rows_sum = jnp.zeros((8, pixels), F32)
    head_sum = jnp.zeros((8, width), F32)
    later = ()
    parcels = [None] * frames
    for frame_no in reversed(range(frames)):
        gates, cells_prev = kept[frame_no]
        lows, grad_cells, sums_part, echo_part, rows_part, head_part = backward_frame(
            owners,
            scalars,
            seen[:, frame_no],
            mine_rows[1, frame_no],
            mine_rows[2, frame_no],
            gates,
            cells_prev,
            norms,
            head,
            looks[frame_no],
            later,
        )
        parcels[frame_no] = lax.all_to_all(lows, "dp", 0, 0)
        sums, echo = sums + sums_part, echo + echo_part
        rows_sum, head_sum = rows_sum + rows_part, head_sum + head_part
        if frame_no > 0:
            sides = None
            if slabs > 1:
                edge = MARGIN * columns
                up = [(s, s - blocks) for s in range(blocks, tiles)]
                down = [(s - blocks, s) for s in range(blocks, tiles)]
                below = lax.ppermute(lows[0, :edge], "tile", up)
                above = lax.ppermute(lows[0, pixels - edge :], "tile", down)
                sides = (above, below)
            pieces = list(
                hidden_gradient(
                    columns, blocks, jnp.reshape(block, (1,)).astype(I32), where, sides, lows, parts
                )
            )
            for k in range(1, blocks):
                pairs = [(j, j ^ k) for j in range(tiles)]
                pieces[k] = lax.ppermute(pieces[k], "tile", pairs)
            patches[frame_no] = patches_of(frame_no, turns[frame_no])
            later = [grad_cells] + pieces

    own_grad = jnp.zeros((8, gate), F32)
    if slabs == 1:
        for frame_no in reversed(range(1, frames)):
            part = patch_gradient(patches[frame_no], [parcels[frame_no]])[0]
            own_grad = part if frame_no == frames - 1 else own_grad + part
    lift_grads = lift_gradients(where, echo, parts, [own_grad])
    pieces = [None] + [all_tiles(p, [own_grad, lift_grads]) for p in parcels[1:]]

    once = (block == 0).astype(F32)
    norm_part = jnp.zeros((2, 4, hidden_dim), F32)
    norm_part = lax.dynamic_update_slice_in_dim(
        norm_part, sums[:2].reshape(2, 4, width), block * width, 2
    )
    head_part = lax.dynamic_update_slice_in_dim(
        jnp.zeros((hidden_dim,), F32), head_sum[0], block * width, 0
    )
    packed = jnp.concatenate(
        [
            norm_part.reshape(-1),
            lift_grads.reshape(-1),
            head_part,
            jnp.sum(rows_sum[:2], axis=1) * once,
        ]
    )
    lanes = 2 * GROUP_SIZE
    packed = jnp.pad(packed, (0, -packed.shape[0] % lanes)).reshape(-1, lanes)
    my_block = jnp.reshape(block, (1,)).astype(I32)

    def final_states(parts, between):
        for k in range(1, blocks):
            parts[k] = lax.ppermute(parts[k], "tile", [(j, j ^ k) for j in range(tiles)])
        got = join_states(my_block, parts, between)
        return list(got)

    devices = owners * tiles
    if slabs == 1:
        own_grad, square = patch_gradient(patches[0], [parcels[0]], own_grad)
        packed = jnp.broadcast_to(jnp.concatenate([packed, square])[None], (devices, packed.shape[0] + 1, lanes))
        parts = split_states(my_block, blocks, hidden, cells, [square])
        bases = [0.0] * (blocks - 1)
        for frame_no in reversed(range(1, frames)):
            got = patch_gradient(patches[frame_no], pieces[frame_no][1:], waits=[packed, parts[0]])
            bases = [b + g for b, g in zip(bases, got)]
        everyone = lax.all_to_all(packed, ("dp", "tile"), 0, 0)
        final = final_states(parts, [bases[-1]])
        pieces[0] = all_tiles(parcels[0], [everyone] + bases)
        bases, late = [own_grad] + bases, [patches[0]] + pieces[0][1:]
    else:
        pieces[0] = all_tiles(parcels[0])
        bases, late = [], []
        for b in range(blocks):
            grad = 0.0
            for frame_no in range(frames):
                piece = [pieces[frame_no][s * blocks + b] for s in range(slabs)]
                piece = jnp.stack(piece, axis=1).reshape(owners * image, gate)
                grad = grad + jnp.dot(patches[frame_no], piece, preferred_element_type=F32)
            bases.append(grad)
        own_grad = bases[0]
        for b in range(1, blocks):
            own_grad = jnp.where(block == b, bases[b], own_grad)
        square = jnp.sum(own_grad * own_grad, axis=0, keepdims=True) * (slab == 0).astype(F32)
        square = square[:, : 2 * GROUP_SIZE] + square[:, 2 * GROUP_SIZE :]
        final = final_states(split_states(my_block, blocks, hidden, cells, []), [])
        packed = jnp.broadcast_to(jnp.concatenate([packed, square])[None], (devices, packed.shape[0] + 1, lanes))
        everyone = lax.all_to_all(packed, ("dp", "tile"), 0, 0)
    correction = 1.0 - jnp.power(0.5, step_count[0].astype(F32))
    kernel_rate = (TAPS * IN_DIM) ** (-0.5)
    smalls = [norm_params, norm_moment, norm_second, end_params, end_moment, end_second] + heads
    out = last_update(
        me,
        jnp.stack([correction, count]),
        everyone,
        smalls,
        bases,
        late,
        (kernels[0], kernel_moment[0], kernel_second[0]),
        kernel_rate,
    )
    return (
        (out[3].reshape(()), out[4].reshape(()))
        + tuple(k[None] for k in out[:3])
        + tuple(out[5:11])
        + tuple(h.reshape(1) for h in out[11:14])
        + tuple(g.reshape(1, 1, tile_rows, columns, hidden_dim) for g in final)
    )


def solution(mesh):
    rows = P("dp", None, "tile", None)
    kern = P(None, "dp", None)
    state = P(None, "dp", "tile", None, None)
    placed = (rows, rows, rows, P("dp"), P(), kern, kern, kern) + (P(),) * 9 + (state, state)
    outs = (P(), P(), kern, kern, kern) + (P(),) * 9 + (state, state)
    return jax.shard_map(
        per_device, mesh=mesh, in_specs=placed, out_specs=outs, check_vma=False
    )
```

```python
import math

import jax
import jax.numpy as jnp
from jax import lax
from jax.experimental import pallas as pl
from jax.experimental.pallas import tpu as pltpu
from jax.sharding import PartitionSpec as P

IN_DIM = 512
KERNEL = 5
GROUP_SIZE = 64
MARGIN = KERNEL // 2
TAPS = KERNEL * KERNEL
ONES_ROW = 32

clip_limit = 0.005
small_rate = 0.1
BF = jnp.bfloat16
F32 = jnp.float32
I32 = jnp.int32
EXACT = lax.Precision.HIGHEST


def spread(x, axes):
    n = lax.axis_size(axes)
    return lax.all_to_all(jnp.broadcast_to(x[None], (n,) + x.shape), axes, 0, 0)


def shape(dims, kind):
    return jax.ShapeDtypeStruct(dims, kind)


def hint(microseconds):
    return pl.CostEstimate(
        flops=int(microseconds * 0.35 * 1e9), bytes_accessed=int(microseconds * 0.35 * 3e6), transcendentals=0
    )


def whole(array):
    dims = array.shape
    return pl.BlockSpec(dims, lambda *unused: (0,) * len(dims))


def after(value, *others):
    def body(*refs):
        pass

    anywhere = pl.BlockSpec(memory_space=pl.ANY)
    return pl.pallas_call(
        body,
        out_shape=shape(value.shape, value.dtype),
        in_specs=[anywhere] * (1 + len(others)),
        out_specs=anywhere,
        input_output_aliases={0: 0},
        name="after",
    )(value, *others)


def columns_kernel(place, first, second, third, fourth, out):
    odd = place[1] == 1
    lower = lax.broadcasted_iota(I32, first.shape, 1) < GROUP_SIZE

    def pair(left, right):
        x, y = left[...], right[...]
        low = jnp.where(odd, pltpu.roll(x, GROUP_SIZE, 1), x)
        high = jnp.where(odd, y, pltpu.roll(y, GROUP_SIZE, 1))
        return jnp.where(lower, low, high).astype(BF)

    out[:, : 2 * GROUP_SIZE] = pair(first, second)
    out[:, 2 * GROUP_SIZE :] = pair(third, fourth)


def own_kernel_columns(kernels, block):
    own, gate_dim = kernels.shape
    lanes = 2 * GROUP_SIZE
    per_quarter = gate_dim // 4 // lanes
    steps = 2 if own % 32 == 0 else 5
    step = own // steps
    place = jnp.stack([block // 2, block % 2]).astype(I32)

    def spec(quarter):
        return pl.BlockSpec((step, lanes), lambda i, where: (i, quarter * per_quarter + where[0]))

    return pl.pallas_call(
        columns_kernel,
        out_shape=shape((own, 4 * GROUP_SIZE), BF),
        grid_spec=pltpu.PrefetchScalarGridSpec(
            num_scalar_prefetch=1,
            grid=(steps,),
            in_specs=[spec(q) for q in range(4)],
            out_specs=pl.BlockSpec((step, 4 * GROUP_SIZE), lambda i, where: (i, 0)),
        ),
        name="columns",
    )(place, kernels, kernels, kernels, kernels)


def group_mean(values):
    n = values.shape[1]
    same = (
        lax.broadcasted_iota(I32, (n, n), 0) // GROUP_SIZE
        == lax.broadcasted_iota(I32, (n, n), 1) // GROUP_SIZE
    )
    mixer = jnp.where(same, 1.0 / GROUP_SIZE, 0.0).astype(F32)
    return jnp.dot(values, mixer, precision=EXACT, preferred_element_type=F32)


def fill_bands(bands, image, columns, mirrored=False):
    pixels, depth = image.shape
    edge = MARGIN * columns
    column = lax.broadcasted_iota(I32, image.shape, 0) % columns
    blank = jnp.zeros((edge, depth), BF)
    for d in range(KERNEL):
        move = (MARGIN - d) if mirrored else (d - MARGIN)
        lanes = slice(d * depth, (d + 1) * depth)
        moved = image if move == 0 else pltpu.roll(image, (-move) % pixels, 0)
        inside = (column + move >= 0) & (column + move < columns)
        bands[edge : edge + pixels, lanes] = jnp.where(inside, moved, 0.0).astype(BF)
        bands[:edge, lanes] = blank
        bands[edge + pixels :, lanes] = blank


def cell_parts(gates, cells_prev, gain, shift):
    width = cells_prev.shape[1]
    centred = gates - group_mean(gates)
    inverse = lax.rsqrt(group_mean(centred * centred) + 1e-05)
    norm = centred * inverse
    normed = norm * gain + shift
    input_gate = jax.nn.sigmoid(normed[:, :width])
    forget_gate = jax.nn.sigmoid(normed[:, width : 2 * width])
    candidate = jnp.tanh(normed[:, 2 * width : 3 * width])
    output_gate = jax.nn.sigmoid(normed[:, 3 * width :])
    cells = forget_gate * cells_prev + input_gate * candidate
    return norm, inverse, input_gate, forget_gate, candidate, output_gate, cells


def forward_kernel(
    columns, first_row, obs, hid, ends, weight, cells_prev, norms, head,
    gates_out, cells_out, hidden_out, low_out, turned_out, seen_out, bands, total, near, arrived,
):
    pixels = total.shape[0]

    def fetch(step):
        return pltpu.make_async_copy(weight.at[step], near.at[step], arrived.at[step])

    for step in range(KERNEL):
        fetch(step).start()
    lifted = (ends[0:1, :] * obs[...] + ends[1:2, :]).astype(BF).astype(F32)
    fill_bands(bands, jnp.concatenate([lifted, hid[...].astype(F32)], axis=1), columns)
    total[...] = jnp.zeros_like(total)

    @pl.loop(0, KERNEL)
    def tap_row(step):
        begin = pl.multiple_of((first_row[0] + step) * columns, columns)
        fetch(step).wait()
        total[...] += jnp.dot(
            bands[pl.ds(begin, pixels), :], near[step], preferred_element_type=F32
        )

    gates = total[...]
    parts = cell_parts(gates, cells_prev[...], norms[0:1, :], norms[1:2, :])
    output_gate, cells = parts[5], parts[6]
    hidden = output_gate * jnp.tanh(cells)
    gates_out[...] = gates
    cells_out[...] = cells
    hidden_out[...] = hidden
    low_out[...] = hidden.astype(BF)
    turned_out[...] = jnp.broadcast_to(jnp.transpose(hidden).astype(BF)[None], turned_out.shape)
    seen_out[...] = lax.dot_general(
        head[...], hidden, (((1,), (1,)), ((), ())), precision=EXACT, preferred_element_type=F32
    )[0:1, :]


def forward_frame(copies, columns, first_row, obs, hid, ends, weight, cells_prev, norms, head):
    pixels, width = cells_prev.shape
    image = hid.shape[0]
    gate = 4 * width
    outs = (
        shape((pixels, gate), F32),
        shape((pixels, width), F32),
        shape((pixels, width), F32),
        shape((pixels, width), BF),
        shape((copies, width, pixels), BF),
        shape((1, pixels), F32),
    )

    def body(*refs):
        forward_kernel(columns, *refs)

    return pl.pallas_call(
        body,
        out_shape=outs,
        grid_spec=pltpu.PrefetchScalarGridSpec(
            num_scalar_prefetch=1,
            grid=(1,),
            in_specs=[
                whole(obs),
                whole(hid),
                whole(ends),
                pl.BlockSpec(memory_space=pl.ANY),
                whole(cells_prev),
                whole(norms),
                whole(head),
            ],
            out_specs=[whole(o) for o in outs],
            scratch_shapes=[
                pltpu.VMEM((image + 2 * MARGIN * columns, KERNEL * IN_DIM), BF),
                pltpu.VMEM((pixels, gate), F32),
                pltpu.VMEM((KERNEL, KERNEL * IN_DIM, gate), BF),
                pltpu.SemaphoreType.DMA((KERNEL,)),
            ],
        ),
        cost_estimate=hint(4),
        name="forward_frame",
    )(
        first_row, obs, hid, ends, weight.reshape(KERNEL, KERNEL * IN_DIM, gate), cells_prev,
        norms, head,
    )


def backward_kernel(last, *refs):
    (scalars, seen, target, valid, gates, cells_prev, norms, head, looks) = refs[:9]
    grad_next, pieces = (None, ()) if last else (refs[9], refs[10:-6])
    low_out, cells_grad, sums_out, echo_out, rows_out, head_out = refs[-6:]
    pixels, width = cells_prev.shape
    gain = norms[0:1, :]
    error = jnp.sum(seen[...], axis=0, keepdims=True) + scalars[0] - target[...]
    weighted = valid[...] * error
    grad_row = 2.0 * weighted / scalars[1]
    rows_out[0:1, :] = grad_row
    rows_out[1:2, :] = weighted * error
    rows_out[2:8, :] = jnp.zeros((6, pixels), F32)
    grad_pred = jnp.transpose(jnp.broadcast_to(grad_row, (2 * GROUP_SIZE, pixels)))[:, :width]

    norm, inverse, input_gate, forget_gate, candidate, output_gate, cells = cell_parts(
        gates[...], cells_prev[...], gain, norms[1:2, :]
    )
    squashed = jnp.tanh(cells)
    grad_hidden = grad_pred * head[0:1, :]
    for piece in pieces:
        grad_hidden = grad_hidden + piece[...]
    head_out[...] = jnp.broadcast_to(
        jnp.sum(grad_pred * (output_gate * squashed), axis=0, keepdims=True), head_out.shape
    )
    grad_cells = grad_hidden * output_gate * (1.0 - squashed * squashed)
    if not last:
        grad_cells = grad_cells + grad_next[...]
    cells_grad[...] = grad_cells * forget_gate
    grad_normed = jnp.concatenate(
        [
            grad_cells * candidate * input_gate * (1.0 - input_gate),
            grad_cells * cells_prev[...] * forget_gate * (1.0 - forget_gate),
            grad_cells * input_gate * (1.0 - candidate * candidate),
            grad_hidden * squashed * output_gate * (1.0 - output_gate),
        ],
        axis=1,
    )
    sums_out[0:1, :] = jnp.sum(grad_normed * norm, axis=0, keepdims=True)
    sums_out[1:2, :] = jnp.sum(grad_normed, axis=0, keepdims=True)
    sums_out[2:8, :] = jnp.zeros((6, 4 * width), F32)
    scaled = grad_normed * gain
    grad_gates = inverse * (scaled - group_mean(scaled) - norm * group_mean(scaled * norm))
    low = grad_gates.astype(BF)
    low_out[...] = jnp.broadcast_to(low[None], low_out.shape)
    echo_out[...] = jnp.dot(
        looks[...], low.astype(F32), precision=EXACT, preferred_element_type=F32
    )


def backward_frame(
    copies, scalars, seen, target, valid, gates, cells_prev, norms, head, looks, later
):
    pixels, width = cells_prev.shape
    gate = 4 * width
    outs = (
        shape((copies, pixels, gate), BF),
        shape((pixels, width), F32),
        shape((8, gate), F32),
        shape((looks.shape[0], gate), F32),
        shape((8, pixels), F32),
        shape((8, width), F32),
    )
    args = [seen, target, valid, gates, cells_prev, norms, head, looks] + list(later)
    last = not later

    def body(*refs):
        backward_kernel(last, *refs)

    return pl.pallas_call(
        body,
        out_shape=outs,
        in_specs=[pl.BlockSpec(memory_space=pltpu.SMEM)] + [whole(a) for a in args],
        out_specs=[whole(o) for o in outs],
        grid=(1,),
        cost_estimate=hint(4),
        name="backward_cell",
    )(scalars, *args)


def hidden_kernel(columns, me, above, low, below, weight, *refs):
    outs, (bands, total, held, near, arrived) = refs[:-5], refs[-5:]
    pixels = low.shape[1]
    blocks, unused, width = held.shape

    def fetch(step):
        return pltpu.make_async_copy(
            weight.at[pl.ds(step * KERNEL, KERNEL), 1], near.at[step], arrived.at[step]
        )

    for step in range(KERNEL):
        fetch(step).start()
    fill_bands(bands, low[0].astype(F32), columns, mirrored=True)
    edge = MARGIN * columns
    if above is not None:
        for side, place in ((above, 0), (below, edge + pixels)):
            image = side[...].astype(F32)
            column = lax.broadcasted_iota(I32, image.shape, 0) % columns
            depth = image.shape[1]
            for d in range(KERNEL):
                move = MARGIN - d
                moved = image if move == 0 else pltpu.roll(image, (-move) % edge, 0)
                inside = (column + move >= 0) & (column + move < columns)
                bands[place : place + edge, d * depth : (d + 1) * depth] = jnp.where(
                    inside, moved, 0.0
                ).astype(BF)
    total[...] = jnp.zeros_like(total)

    @pl.loop(0, KERNEL)
    def tap_row(step):
        begin = pl.multiple_of((KERNEL - 1 - step) * columns, columns)
        fetch(step).wait()
        taps = jnp.concatenate([near[step, d] for d in range(KERNEL)], axis=1)
        total[...] += lax.dot_general(
            bands[pl.ds(begin, pixels), :],
            taps,
            (((1,), (1,)), ((), ())),
            preferred_element_type=F32,
        )

    for b in range(blocks):
        held[jnp.bitwise_xor(b, me[0])] = total[:, b * width : (b + 1) * width]
    for k in range(blocks):
        outs[k][...] = held[k]


def hidden_gradient(columns, blocks, me, sides, low, weight):
    unused, pixels, gate = low.shape
    hidden_dim = weight.shape[1] // 2
    halves = weight.reshape(TAPS, 2, hidden_dim, gate)
    width = hidden_dim // blocks
    outs = (shape((pixels, width), F32),) * blocks
    args = [low] if sides is None else [sides[0], low, sides[1]]
    specs = [pl.BlockSpec((1,) + a.shape[1:], lambda *i: (0, 0, 0)) if a is low else whole(a) for a in args]

    def body(me_ref, *refs):
        if sides is None:
            hidden_kernel(columns, me_ref, None, refs[0], None, *refs[1:])
        else:
            hidden_kernel(columns, me_ref, *refs)

    return pl.pallas_call(
        body,
        out_shape=outs,
        grid_spec=pltpu.PrefetchScalarGridSpec(
            num_scalar_prefetch=1,
            grid=(1,),
            in_specs=specs + [pl.BlockSpec(memory_space=pl.ANY)],
            out_specs=[whole(o) for o in outs],
            scratch_shapes=[
                pltpu.VMEM((pixels + 2 * MARGIN * columns, KERNEL * gate), BF),
                pltpu.VMEM((pixels, hidden_dim), F32),
                pltpu.VMEM((blocks, pixels, width), F32),
                pltpu.VMEM((KERNEL, KERNEL, hidden_dim, gate), BF),
                pltpu.SemaphoreType.DMA((KERNEL,)),
            ],
        ),
        cost_estimate=hint(4),
        name="hidden_gradient",
    )(me, *args, halves)


def patches_kernel(columns, slabs, tiles, places, obs, ends, *refs):
    hid, (out, moves, patches, held) = refs[:tiles], refs[tiles:]
    own, image = out.shape
    span = moves.shape[0]
    for k in range(tiles):
        held[k] = hid[k][0]

    @pl.when(pl.program_id(0) == 0)
    def start():
        source = lax.broadcasted_iota(I32, (image, image), 0)
        target = lax.broadcasted_iota(I32, (image, image), 1)
        for k in range(span):
            row_off, col_off = places[2 + 2 * k], places[3 + 2 * k]
            column = target % columns + col_off
            hit = source == target + row_off * columns + col_off
            hit = hit & (column >= 0) & (column < columns)
            moves[k] = jnp.where(hit, 1.0, 0.0).astype(BF)

    lifted = (ends[:, 0:1] * obs[0] + ends[:, 1:2]).astype(BF)
    blocks = tiles // slabs
    parts = [lifted]
    for b in range(blocks):
        piece = [held[jnp.bitwise_xor(s * blocks + b, places[1])] for s in range(slabs)]
        parts.append(piece[0] if slabs == 1 else jnp.concatenate(piece, axis=1))
    joined = jnp.concatenate(parts, axis=0)
    for k in range(span):
        patches[k * IN_DIM : (k + 1) * IN_DIM, :] = jnp.dot(
            joined, moves[k], preferred_element_type=F32
        ).astype(BF)
    skip = pl.multiple_of(places[0], 16)
    out[...] = patches[pl.ds(skip, own), :]


def owned_patches(columns, slabs, own, span, places, obs, hid, ends):
    owners, unused, image = obs.shape
    tiles, (unused_too, width, pixels) = len(hid), hid[0].shape

    def body(*refs):
        patches_kernel(columns, slabs, tiles, *refs)

    return pl.pallas_call(
        body,
        out_shape=shape((own, owners * image), BF),
        grid_spec=pltpu.PrefetchScalarGridSpec(
            num_scalar_prefetch=1,
            grid=(owners,),
            in_specs=[
                pl.BlockSpec((1, 1, image), lambda s, where: (s, 0, 0)),
                whole(ends),
            ]
            + [pl.BlockSpec((1, width, pixels), lambda s, where: (s, 0, 0))] * tiles,
            out_specs=pl.BlockSpec((own, image), lambda s, where: (0, s)),
            scratch_shapes=[
                pltpu.VMEM((span, image, image), BF),
                pltpu.VMEM((span * IN_DIM, image), BF),
                pltpu.VMEM((tiles, width, pixels), BF),
            ],
        ),
        cost_estimate=hint(9),
        name="owned_patches",
    )(places, obs, ends, *hid)


def adamw(weight, moment, second, grad, rate, correction):
    moment_new = 0.5 * moment + 0.5 * grad
    second_new = 0.5 * second + 0.5 * grad * grad
    update = moment_new / correction / (jnp.sqrt(second_new / correction) + 1e-08)
    return (weight - rate * (update + 0.01 * weight), moment_new, second_new)


def rows_at_once(own):
    return 16 * math.gcd(own // 16, 25)


def patch_dot(patch, pieces):
    flat = [p[...].reshape(patch.shape[1], p.shape[2]) for p in pieces]
    signal = flat[0] if len(flat) == 1 else jnp.concatenate(flat, axis=1)
    return jnp.dot(patch[...], signal, preferred_element_type=F32)


def gradient_kernel(blocks, squared, patch, *refs):
    pieces, refs = refs[:blocks], refs[blocks:]
    grad = patch_dot(patch, pieces)
    gate = pieces[0].shape[2]
    if squared:
        base, grad_out, square_out = refs
        grad = grad + base[...]

        @pl.when(pl.program_id(0) == 0)
        def start():
            square_out[...] = jnp.zeros_like(square_out)

        lanes = square_out.shape[1]
        square = grad * grad
        square = square[:, :lanes] + square[:, lanes:]
        square_out[...] += jnp.sum(square, axis=0, keepdims=True)
        grad_out[...] = grad
    else:
        for k in range(blocks):
            refs[k][...] = grad[:, k * gate : (k + 1) * gate]


def patch_gradient(patch, pieces, base=None, waits=()):
    own, gate = patch.shape[0], pieces[0].shape[2]
    step = own // 2
    rows = pl.BlockSpec((step, gate), lambda i: (i, 0))
    outs = [shape((own, gate), F32) for p in pieces]
    out_specs = [rows] * len(pieces)
    args = [patch] + list(pieces)
    in_specs = [pl.BlockSpec((step, patch.shape[1]), lambda i: (i, 0))] + [whole(p) for p in pieces]
    if base is not None:
        args, in_specs = args + [base], in_specs + [rows]
        outs = outs + [shape((1, gate // 2), F32)]
        out_specs = out_specs + [pl.BlockSpec((1, gate // 2), lambda i: (0, 0))]

    n = len(args)
    args, in_specs = args + list(waits), in_specs + [pl.BlockSpec(memory_space=pl.ANY)] * len(waits)

    def body(*refs):
        gradient_kernel(len(pieces), base is not None, *refs[:n], *refs[n + len(waits) :])

    return pl.pallas_call(
        body,
        out_shape=tuple(outs),
        grid=(own // step,),
        in_specs=in_specs,
        out_specs=out_specs,
        compiler_params=pltpu.CompilerParams(vmem_limit_bytes=60 << 20),
        cost_estimate=hint(3 + 2 * len(pieces)),
        name="patch_gradient",
    )(*args)


def small_update(scalars, everyone, triples, factor_row, smalls_out, measures_out):
    total = jnp.sum(everyone[...], axis=0)
    lanes = total.shape[1]
    gate_dim, hidden_dim = triples[0].shape[2], triples[3].shape[1]
    norm_rows = 2 * gate_dim // lanes
    end_rows = 3 * hidden_dim // lanes
    last = norm_rows + end_rows
    row = lax.broadcasted_iota(I32, total.shape, 0)
    lane = lax.broadcasted_iota(I32, total.shape, 1)
    wide = (row < last) | ((row == last) & (lane == 0))
    alone = row == last + 1
    squares = jnp.where(wide, total * total, jnp.where(alone, total, 0.0))
    grad_norm = jnp.sqrt(jnp.sum(jnp.sum(squares, axis=0, keepdims=True), axis=1, keepdims=True))
    factor = clip_limit / jnp.maximum(grad_norm, clip_limit)
    factor_row[...] = jnp.broadcast_to(factor, factor_row.shape)
    measures_out[0][...] = total[last : last + 1, 1:2] / scalars[1]
    measures_out[1][...] = grad_norm

    def line(begin, length):
        return jnp.concatenate([total[r : r + 1, :] for r in range(begin, begin + length)], axis=1)

    def update(place, grad, index):
        found = [t[index] for t in triples[place : place + 3]]
        got = adamw(*found, grad * factor, small_rate, scalars[0])
        for out, value in zip(smalls_out[place : place + 3], got):
            out[index] = value

    for r in range(2):
        update(0, line(r * norm_rows // 2, norm_rows // 2), r)
    for r in range(3):
        update(3, line(norm_rows + r * end_rows // 3, end_rows // 3), slice(r, r + 1))
    update(6, total[last : last + 1, 0:1], slice(0, 1))


def last_kernel(blocks, extra, rate, me, scalars, everyone, *refs):
    triples, refs = refs[:9], refs[9:]
    bases, refs = refs[:blocks], refs[blocks:]
    pieces, refs = refs[:extra], refs[extra:]
    held, factor_row = refs[-2:]
    weight, moment, second, weight_out, moment_out, second_out = refs[:6]
    measures_out, smalls_out = refs[6:8], refs[8:17]

    @pl.when(pl.program_id(0) == 0)
    def start():
        small_update(scalars, everyone, triples, factor_row, smalls_out, measures_out)

    for k in range(blocks):
        held[k] = bases[k][...]
    if extra:
        patch, pieces = pieces[0], pieces[1:]
        grad = patch_dot(patch, pieces)
        gate = held.shape[2]
        for k in range(1, blocks):
            held[k] += grad[:, (k - 1) * gate : k * gate]
    width = held.shape[2] // 4
    placed = [held[jnp.bitwise_xor(b, me[0])] for b in range(blocks)]
    for q in range(4):
        grad = jnp.concatenate([p[:, q * width : (q + 1) * width] for p in placed], axis=1)
        cols = slice(q * blocks * width, (q + 1) * blocks * width)
        weight_out[:, cols], moment_out[:, cols], second_out[:, cols] = adamw(
            weight[:, cols], moment[:, cols], second[:, cols], grad * factor_row[...], rate,
            scalars[0],
        )


def last_update(me, scalars, everyone, smalls, bases, late, kernel_triple, rate):
    own, gate_dim = kernel_triple[0].shape
    blocks = len(bases)
    step = rows_at_once(own)
    gate = gate_dim // blocks
    wide = pl.BlockSpec((step, gate_dim), lambda i, where: (i, 0))
    thin = pl.BlockSpec((step, gate), lambda i, where: (i, 0))
    late_specs = []
    if late:
        late_specs = [pl.BlockSpec((step, late[0].shape[1]), lambda i, where: (i, 0))]
        late_specs += [whole(p) for p in late[1:]]
    measures = [shape((1, 1), F32)] * 2

    def body(*refs):
        n = 3 + 9 + blocks + len(late)
        ins, outs = refs[: n + 3], refs[n + 3 :]
        last_kernel(blocks, len(late), rate, *ins, *outs)

    return pl.pallas_call(
        body,
        out_shape=tuple([shape((own, gate_dim), F32)] * 3 + measures + [shape(t.shape, F32) for t in smalls]),
        grid_spec=pltpu.PrefetchScalarGridSpec(
            num_scalar_prefetch=1,
            grid=(own // step,),
            in_specs=[pl.BlockSpec(memory_space=pltpu.SMEM), whole(everyone)]
            + [whole(t) for t in smalls]
            + [thin] * blocks
            + late_specs
            + [wide] * 3,
            out_specs=[wide] * 3 + [whole(m) for m in measures] + [whole(t) for t in smalls],
            scratch_shapes=[
                pltpu.VMEM((blocks, step, gate), F32),
                pltpu.VMEM((1, gate_dim // 4), F32),
            ],
        ),
        compiler_params=pltpu.CompilerParams(vmem_limit_bytes=60 << 20),
        cost_estimate=hint(22),
        name="last_update",
    )(me, scalars, everyone, *smalls, *bases, *late, *kernel_triple)


def split_low(values):
    high = values.astype(BF)
    return high, (values - high.astype(F32)).astype(BF)


def per_device(
    observed,
    targets,
    pixel_mask,
    lengths,
    step_count,
    kernels,
    kernel_moment,
    kernel_second,
    norm_params,
    norm_moment,
    norm_second,
    end_params,
    end_moment,
    end_second,
    head_bias,
    head_moment,
    head_second,
    hidden_init,
    cells_init,
):
    tiles, owners = lax.axis_size("tile"), lax.axis_size("dp")
    streams, frames, tile_rows, columns = observed.shape
    height = tile_rows * tiles
    hidden_dim = end_params.shape[1]
    gate_dim = 4 * hidden_dim
    blocks = math.gcd(tiles, hidden_dim // GROUP_SIZE)
    slabs = tiles // blocks
    rows = height // slabs
    width = hidden_dim // blocks
    gate = 4 * width
    pixels, image = rows * columns, height * columns
    own = kernels.shape[1]
    assert streams == 1 and width == GROUP_SIZE and own % 80 == 0 and pixels == gate
    tile = lax.axis_index("tile")
    owner = lax.axis_index("dp")
    block, slab = tile % blocks, tile // blocks
    first_row = slab * rows
    groups = None
    if slabs > 1:
        groups = [[s * blocks + b for b in range(blocks)] for s in range(slabs)]

    weight = lax.all_gather(own_kernel_columns(kernels[0], block), "dp", axis=0, tiled=True)
    weight = weight.reshape(TAPS, IN_DIM, gate)

    frame_ids = lax.broadcasted_iota(I32, (1, frames), 1)
    counted = (frame_ids < lengths[:, None]).astype(F32)
    valid = pixel_mask.astype(F32) * counted[:, :, None, None]
    small = spread(jnp.stack([observed[0], targets[0], valid[0]]), ("dp", "tile"))
    small = small.reshape(owners, tiles, 3, frames, tile_rows * columns)
    small = small.transpose(2, 3, 0, 1, 4).reshape(3, frames, owners, image)
    count = jnp.maximum(jnp.sum(small[2]), 1.0)
    obs_all = small[0]
    mine = lax.dynamic_slice_in_dim(small, owner, 1, 2)
    mine_rows = lax.dynamic_slice_in_dim(mine, first_row * columns, pixels, 3)

    def own_columns(values):
        shaped = values.reshape(values.shape[:-1] + (4, hidden_dim))
        part = lax.dynamic_slice_in_dim(shaped, block * width, width, values.ndim)
        return part.reshape(values.shape[:-1] + (gate,))

    norms = own_columns(norm_params[:, 0])
    head = lax.dynamic_slice_in_dim(end_params[2], block * width, width, 0)
    head = jnp.broadcast_to(head[None], (8, width))
    ends = end_params[:2]
    ends_turned = ends.T

    me = jnp.reshape(block if slabs == 1 else jnp.zeros_like(block), (1,)).astype(I32)

    def all_tiles(values, between=()):
        if slabs > 1:
            got = lax.all_gather(values, "tile")
            return [got[k] for k in range(tiles)]
        held, order, stride = [values], [0], tiles // 2
        while stride:
            pairs = [(j, j ^ stride) for j in range(tiles)]
            held = held + [lax.ppermute(h, "tile", pairs) for h in held]
            if between and stride > 1:
                held[1:] = [after(h, *between) for h in held[1:]]
            order = order + [k ^ stride for k in order]
            stride //= 2
        return [held[order.index(k)] for k in range(tiles)]

    span = max((own * (i + 1) - 1) // IN_DIM - own * i // IN_DIM + 1 for i in range(owners))
    first_tap = jnp.minimum(owner * own // IN_DIM, TAPS - span)
    places = [owner * own - first_tap * IN_DIM, me[0]]
    for k in range(span):
        places += [(first_tap + k) // KERNEL - MARGIN, (first_tap + k) % KERNEL - MARGIN]
    places = jnp.stack(places).astype(I32)

    def patches_of(frame_no, hid):
        obs_rows = obs_all[frame_no].reshape(owners, 1, image)
        return owned_patches(columns, slabs, own, span, places, obs_rows, hid, ends_turned)

    states = jnp.stack([hidden_init[0, 0], cells_init[0, 0]])
    states = states.reshape(2, tile_rows * columns, blocks, width).transpose(2, 0, 1, 3)
    states = lax.all_to_all(states, "tile", 0, 0, axis_index_groups=groups)
    states = states.transpose(1, 0, 2, 3).reshape(2, pixels, width)
    low = states[0].astype(BF)
    cells = states[1]
    patches = [None] * frames
    patches[0] = patches_of(0, all_tiles(spread(low.T, "dp")))

    def whole_hidden(values):
        got = lax.all_gather(values, "tile").reshape(slabs, blocks, pixels, width)
        return got.transpose(0, 2, 1, 3).reshape(image, hidden_dim)

    weight, patches[0] = lax.optimization_barrier((weight, patches[0]))
    first = jnp.reshape(first_row, (1,)).astype(I32)
    kept, seen, turns = [], [], [None] * frames
    for frame_no in range(frames):
        obs_column = mine[0, frame_no].reshape(image, 1)
        gates, cells_next, hidden, low_next, turned, seen_part = forward_frame(
            owners, columns, first, obs_column, whole_hidden(low), ends, weight, cells, norms, head
        )
        kept.append((gates, cells))
        cells, low = cells_next, low_next
        seen.append(seen_part[0])
        if frame_no + 1 < frames:
            turns[frame_no + 1] = lax.all_to_all(turned, "dp", 0, 0)
    seen = lax.all_gather(jnp.stack(seen), "tile", axis_index_groups=groups)
    seen, turns[1:] = lax.optimization_barrier((seen, turns[1:]))
    turns[1:] = [all_tiles(t) for t in turns[1:]]
    scalars = jnp.stack([head_bias[0], count])

    padded = jnp.pad(
        jnp.stack([mine[0, :, 0], jnp.ones_like(mine[0, :, 0])], axis=1).reshape(
            frames, 2, height, columns
        ),
        ((0, 0), (0, 0), (MARGIN, MARGIN), (MARGIN, MARGIN)),
    )
    padded = lax.dynamic_slice_in_dim(padded, first_row, rows + 2 * MARGIN, 2)
    looks = jnp.stack(
        [
            padded[:, :, a : a + rows, b : b + columns].reshape(frames, 2, pixels)
            for a in range(KERNEL)
            for b in range(KERNEL)
        ],
        axis=2,
    )
    looks = jnp.pad(looks, ((0, 0), (0, 0), (0, ONES_ROW - TAPS), (0, 0)))
    looks = looks.reshape(frames, 2 * ONES_ROW, pixels)

    sums = jnp.zeros((8, gate), F32)
    echo = jnp.zeros((2 * ONES_ROW, gate), F32)
    rows_sum = jnp.zeros((8, pixels), F32)
    head_sum = jnp.zeros((8, width), F32)
    later = ()
    parcels = [None] * frames
    for frame_no in reversed(range(frames)):
        gates, cells_prev = kept[frame_no]
        lows, grad_cells, sums_part, echo_part, rows_part, head_part = backward_frame(
            owners,
            scalars,
            seen[:, frame_no],
            mine_rows[1, frame_no],
            mine_rows[2, frame_no],
            gates,
            cells_prev,
            norms,
            head,
            looks[frame_no],
            later,
        )
        parcels[frame_no] = lax.all_to_all(lows, "dp", 0, 0)
        sums, echo = sums + sums_part, echo + echo_part
        rows_sum, head_sum = rows_sum + rows_part, head_sum + head_part
        if frame_no > 0:
            sides = None
            if slabs > 1:
                edge = MARGIN * columns
                up = [(s, s - blocks) for s in range(blocks, tiles)]
                down = [(s - blocks, s) for s in range(blocks, tiles)]
                below = lax.ppermute(lows[0, :edge], "tile", up)
                above = lax.ppermute(lows[0, pixels - edge :], "tile", down)
                sides = (above, below)
            pieces = list(
                hidden_gradient(
                    columns, blocks, jnp.reshape(block, (1,)).astype(I32), sides, lows, weight
                )
            )
            for k in range(1, blocks):
                pairs = [(j, j ^ k) for j in range(tiles)]
                pieces[k] = lax.ppermute(pieces[k], "tile", pairs)
            patches[frame_no] = patches_of(frame_no, turns[frame_no])
            later = [grad_cells] + pieces

    own_grad = jnp.zeros((8, gate), F32)
    if slabs == 1:
        for frame_no in reversed(range(1, frames)):
            part = patch_gradient(patches[frame_no], [parcels[frame_no]])[0]
            own_grad = part if frame_no == frames - 1 else own_grad + part
    echo = after(echo, own_grad)
    lift_kernel = weight[:, :hidden_dim]
    echoes = echo.reshape(2, ONES_ROW, gate)[:, :TAPS]
    lift_grads = sum(
        jnp.einsum("ktg,tcg->kc", part, lift_kernel, preferred_element_type=F32)
        for part in split_low(echoes)
    )

    pieces = [None] + [all_tiles(p, [own_grad, lift_grads]) for p in parcels[1:]]

    states = after(jnp.stack([hidden, cells]), own_grad)
    states = states.reshape(2, blocks, tile_rows * columns, width)
    final = []
    for k in range(blocks):
        part = lax.dynamic_slice_in_dim(states, jnp.bitwise_xor(block, k), 1, 1)
        if k:
            part = lax.ppermute(part, "tile", [(j, j ^ k) for j in range(tiles)])
        final.append(part)
    final = jnp.concatenate(final, axis=1)
    final = jnp.take(final, jnp.bitwise_xor(jnp.arange(blocks), block), axis=1)
    final = final.transpose(0, 2, 1, 3).reshape(2, 1, 1, tile_rows, columns, hidden_dim)
    once = (block == 0).astype(F32)
    norm_part = jnp.zeros((2, 4, hidden_dim), F32)
    norm_part = lax.dynamic_update_slice_in_dim(
        norm_part, sums[:2].reshape(2, 4, width), block * width, 2
    )
    head_part = lax.dynamic_update_slice_in_dim(
        jnp.zeros((hidden_dim,), F32), head_sum[0], block * width, 0
    )
    packed = jnp.concatenate(
        [
            norm_part.reshape(-1),
            lift_grads.reshape(-1),
            head_part,
            jnp.sum(rows_sum[:2], axis=1) * once,
        ]
    )
    lanes = 2 * GROUP_SIZE
    packed = jnp.pad(packed, (0, -packed.shape[0] % lanes)).reshape(-1, lanes)
    devices = owners * tiles
    if slabs == 1:
        own_grad, square = patch_gradient(patches[0], [parcels[0]], own_grad, waits=[final])
        packed = jnp.broadcast_to(jnp.concatenate([packed, square])[None], (devices, packed.shape[0] + 1, lanes))
        bases = [0.0] * (blocks - 1)
        for frame_no in reversed(range(1, frames)):
            got = patch_gradient(patches[frame_no], pieces[frame_no][1:], waits=[packed])
            bases = [b + g for b, g in zip(bases, got)]
        everyone = lax.all_to_all(packed, ("dp", "tile"), 0, 0)
        pieces[0] = all_tiles(parcels[0], [everyone] + bases)
        bases, late = [own_grad] + bases, [patches[0]] + pieces[0][1:]
    else:
        pieces[0] = all_tiles(parcels[0])
        bases, late = [], []
        for b in range(blocks):
            grad = 0.0
            for frame_no in range(frames):
                piece = [pieces[frame_no][s * blocks + b] for s in range(slabs)]
                piece = jnp.stack(piece, axis=1).reshape(owners * image, gate)
                grad = grad + jnp.dot(patches[frame_no], piece, preferred_element_type=F32)
            bases.append(grad)
        own_grad = bases[0]
        for b in range(1, blocks):
            own_grad = jnp.where(block == b, bases[b], own_grad)
        square = jnp.sum(own_grad * own_grad, axis=0, keepdims=True) * (slab == 0).astype(F32)
        square = square[:, : 2 * GROUP_SIZE] + square[:, 2 * GROUP_SIZE :]
        packed = jnp.broadcast_to(jnp.concatenate([packed, square])[None], (devices, packed.shape[0] + 1, lanes))
        everyone = lax.all_to_all(packed, ("dp", "tile"), 0, 0)
    correction = 1.0 - jnp.power(0.5, step_count[0].astype(F32))
    kernel_rate = (TAPS * IN_DIM) ** (-0.5)
    heads = [h.reshape(1, 1) for h in (head_bias, head_moment, head_second)]
    smalls = [norm_params, norm_moment, norm_second, end_params, end_moment, end_second] + heads
    out = last_update(
        me,
        jnp.stack([correction, count]),
        everyone,
        smalls,
        bases,
        late,
        (kernels[0], kernel_moment[0], kernel_second[0]),
        kernel_rate,
    )
    return (
        (out[3].reshape(()), out[4].reshape(()))
        + tuple(k[None] for k in out[:3])
        + tuple(out[5:11])
        + tuple(h.reshape(1) for h in out[11:14])
        + (final[0], final[1])
    )


def solution(mesh):
    rows = P("dp", None, "tile", None)
    kern = P(None, "dp", None)
    state = P(None, "dp", "tile", None, None)
    placed = (rows, rows, rows, P("dp"), P(), kern, kern, kern) + (P(),) * 9 + (state, state)
    outs = (P(), P(), kern, kern, kern) + (P(),) * 9 + (state, state)
    return jax.shard_map(
        per_device, mesh=mesh, in_specs=placed, out_specs=outs, check_vma=False
    )
```
